256 devices in a mesh: fsdp: 8 (over x, core), seq: 32 (over y, z).
Axes of the slice: x: 4, y: 4, z: 8, core: 2. Of those that a mesh axis runs over, the one named last changes fastest.
Arguments:
- tokens: bfloat16 [131072, 2048], P(('fsdp', 'seq')), may hold values from -42 to 42
- qkv_weight: bfloat16 [2048, 3072], P('seq', 'fsdp'), as said below
- out_weight: bfloat16 [1024, 2048], P('seq', 'fsdp'), may hold values from -0.1875 to 0.1875
- adapter_down: bfloat16 [64, 16, 2048], P('seq'), may hold values from -0.125 to 0.125
- adapter_up: bfloat16 [64, 16, 2048], P('seq'), may hold values from -1.5 to 1.5
- lengths: int32 [8, 16], replicated, may hold values from 1 to 1536, 16384 in all within a row
- adapter_ids: int32 [8, 16], replicated, may hold values from 0 to 63
- adapter_slot: int32 [64], replicated, may hold values from 0 to 63, each once
Outputs:
- attn_out: bfloat16 [131072, 2048], P(('fsdp', 'seq'))
The draws below stay inside these ranges and needn't reach their ends.
Inputs may be any that keep to these rules, and one draw needn't show every extreme that they name: Each row gives the lengths of the 16 requests of one group; a row sums to 16384, and its longest request has exactly 1536 tokens. `adapter_slot`: each slot holds exactly one adapter. `qkv_weight`: entries are of order 1 / sqrt(2048), in some heads' query and key columns up to several times that.
All inputs are finite; a program needn't handle non-finite values.
Results may differ from the reference program's by a relative error of at most 0.023.
Values may be sent and summed in bfloat16 or wider, within the bound.
A program may use at most 128 MiB of HBM per device.

```python
import math
import jax
import jax.numpy as jnp
import numpy as np
from jax import lax

D = 2048
HEADS = 4
HS = 256
RANK = 16
ADAPTERS = 64
SPAN = 3
TOK_DEV = 512
REQS = 16
GROUP = 16384
MAXLEN = 1536
TOKENS = 131072
N_FSDP = 8
N_SEQ = 32


def draw_tokens(key, part):
    first, second, third = jax.random.split(key, 3)
    row_scale = jnp.exp(jax.random.uniform(second, (TOKENS, 1), jnp.float32, 0.0, math.log(3.2)))
    column_scale = jnp.exp(jax.random.uniform(third, (1, D), jnp.float32, 0.0, math.log(3.2)))
    value_vectors = jnp.clip(jax.random.normal(first, (TOKENS, D), jnp.float32), -4.0, 4.0) * row_scale * column_scale
    return value_vectors.astype(jnp.bfloat16)


def draw_qkv_weight(key, part):
    first = jax.random.fold_in(key, 0)
    heads_width_total = HEADS * HS
    drawn = jnp.clip(jax.random.normal(first, (D, 3 * heads_width_total), jnp.float32), -4.0, 4.0) * D ** (-0.5)
    value_vectors = drawn
    return value_vectors.astype(jnp.bfloat16)


def place_ends(values, stream_key, smallest, top_value):
    spot = [jax.random.randint(jax.random.fold_in(stream_key, axis), (), 0, length) for axis, length in enumerate(values.shape)]
    main_axis = values.shape.index(max(values.shape))
    neighbour = spot[:main_axis] + [(spot[main_axis] + 1) % values.shape[main_axis]] + spot[main_axis + 1:]
    return values.at[tuple(spot)].set(smallest).at[tuple(neighbour)].set(top_value)


def levels(key, dims, cuts, least, largest):
    level = 1.0
    for dim, shards_of in cuts:
        draws = jax.random.uniform(jax.random.fold_in(jax.random.fold_in(key, 6), dim), (shards_of,), jnp.float32, least / len(cuts), largest / len(cuts))
        level = level * jnp.repeat(jnp.exp(draws), dims[dim] // shards_of).reshape((-1,) + (1,) * (len(dims) - 1 - dim))
    return level


def cumulative_ranks(amount, lean):
    loads = [(1 << 20) // math.isqrt(rank ** lean) + 1 for rank in range(1, amount + 1)]
    width = 1 + sum(loads) // (1 << 30)
    return np.cumsum(np.array([max(1, weight // width) for weight in loads]))


def skewed_ids(stream_key, dims, number_of, slope):
    listing = cumulative_ranks(number_of, slope)
    ticket = jax.random.randint(jax.random.fold_in(stream_key, 1), dims, 0, int(listing[number_of - 1]))
    standing = jnp.searchsorted(jnp.asarray(listing, jnp.int32), ticket, side="right")
    return jax.random.permutation(jax.random.fold_in(stream_key, 2), number_of)[standing].astype(jnp.int32)


def length_profile(count, total, limit, skew):
    loads = [(1 << 20) // math.isqrt(grade ** skew) + 1 for grade in range(2, count + 1)]
    rest, counts = total - limit - (count - 1), [1] * (count - 1)
    while rest > 0:
        movable = [i for i in range(count - 1) if counts[i] < limit]
        whole, remaining = sum([loads[i] for i in movable]), rest
        for i in movable:
            extra = min(limit - counts[i], max(1, remaining * loads[i] // whole), rest)
            counts[i] = counts[i] + extra
            rest = rest - extra
    return np.array([limit] + counts)


def uneven_parts(own_key, amount, total, most, skew):
    if amount == 2:
        one = jax.random.randint(own_key, (), max(1, total - most), min(most, total - 1) + 1)
        return jnp.stack([one, total - one])
    sizes = jnp.asarray(length_profile(amount, total, most, skew), jnp.int32)
    pairs = (amount - 1) // 2
    giver, receiver = sizes[1:1 + 2 * pairs:2], sizes[2:2 + 2 * pairs:2]
    margin = jnp.minimum(giver - 1, most - receiver)
    shifted = jax.random.randint(jax.random.fold_in(own_key, 1), (pairs,), 0, 1 << 20) % (margin + 1)
    sizes = sizes.at[1:1 + 2 * pairs:2].set(giver - shifted).at[2:2 + 2 * pairs:2].set(receiver + shifted)
    return sizes[jax.random.permutation(jax.random.fold_in(own_key, 2), amount)]


def bell_draw(stream_key, shape, scale, bound, cuts=(), held_as=jnp.bfloat16):
    result = jax.random.normal(stream_key, shape, jnp.float32) * scale
    if len(cuts) > 0:
        result = levels(stream_key, shape, cuts, -0.22, 0.18) * result
    return jnp.clip(result, min=-bound, max=bound).astype(held_as)


def setup_inputs(seed: int = 0) -> dict:
    key_of = jax.random.split(jax.random.key(seed), 9)
    return {
        "tokens": draw_tokens(jax.random.fold_in(key_of[8], 71), 0),
        "qkv_weight": draw_qkv_weight(jax.random.fold_in(key_of[8], 71), 0),
        "out_weight": bell_draw(key_of[2], (HEADS * HS, D), (HEADS * HS) ** -0.5, 0.1875, ((0, 32), (1, 8))),
        "adapter_down": bell_draw(key_of[3], (ADAPTERS, RANK, D), D ** -0.5, 0.125, ((0, 32),)),
        "adapter_up": bell_draw(key_of[4], (ADAPTERS, RANK, 2 * HEADS * HS), RANK ** -0.5, 1.5, ((0, 32),)),
        "lengths": jax.vmap(lambda own: uneven_parts(own, REQS, GROUP, MAXLEN, 2))(jax.random.split(key_of[5], N_FSDP)).reshape((N_FSDP, REQS)).astype(jnp.int32),
        "adapter_ids": place_ends(skewed_ids(key_of[6], (N_FSDP, REQS), ADAPTERS, 2), jax.random.fold_in(key_of[6], 3), 0, ADAPTERS - 1).astype(jnp.int32),
        "adapter_slot": jax.random.permutation(key_of[7], ADAPTERS).astype(jnp.int32),
    }


eps_norm = 1e-05
adapter_scale_factor = 0.5

def layer_norm(token_rows):
    value_vectors = token_rows.astype(jnp.float32)
    average = lax.optimization_barrier(jnp.mean(value_vectors, axis=-1, keepdims=True))
    centred = value_vectors - average
    variance = lax.optimization_barrier(jnp.mean(centred * centred, axis=-1, keepdims=True))
    return (centred * lax.rsqrt(variance + eps_norm)).astype(jnp.bfloat16)

def request_info(length_row, position):
    row_ends = jnp.cumsum(length_row).astype(jnp.int32)
    request = lax.optimization_barrier(jnp.sum((position[:, None] >= row_ends[None, :]).astype(jnp.int32), axis=1))
    onehot = (request[:, None] == jnp.arange(length_row.shape[0], dtype=jnp.int32)[None, :]).astype(jnp.int32)
    begins = lax.optimization_barrier(jnp.sum(onehot * (row_ends - length_row)[None, :], axis=1))
    return (request, onehot, position - begins)

def rotate(head_rows, position):
    rotary = head_rows.shape[-1] // 4
    halfway = rotary // 2
    inverse = 10000.0 ** (-2.0 * jnp.arange(halfway, dtype=jnp.float32) / rotary)
    angles = position.astype(jnp.float32)[:, None] * inverse[None, :]
    cosine = jnp.cos(angles)[:, None, :]
    sine_part = jnp.sin(angles)[:, None, :]
    leading = head_rows[..., :halfway]
    trailing = head_rows[..., halfway:rotary]
    return jnp.concatenate([leading * cosine - trailing * sine_part, trailing * cosine + leading * sine_part, head_rows[..., rotary:]], axis=-1)

def reference(tokens, qkv_weight, out_weight, adapter_down, adapter_up, lengths, adapter_ids, adapter_slot):
    heads_width_total = HEADS * HS
    group_size = TOK_DEV * N_SEQ
    block_total = TOKENS // TOK_DEV
    positions = jnp.tile(jnp.arange(group_size, dtype=jnp.int32)[None, :], (N_FSDP, 1))
    request, onehot, offsets = jax.vmap(request_info)(lengths, positions)
    adapter = lax.optimization_barrier(jnp.sum(onehot * adapter_ids[:, None, :], axis=2)).reshape(-1)
    token_slot = adapter_slot[adapter]
    global_request = (request + REQS * jnp.arange(N_FSDP, dtype=jnp.int32)[:, None]).reshape(-1).astype(jnp.int32)
    offsets = offsets.reshape(-1).astype(jnp.int32)
    normed = layer_norm(tokens)

    def project_block(block_index):
        first_row = (block_index * TOK_DEV).astype(jnp.int32)
        normed_block = lax.dynamic_slice_in_dim(normed, first_row, TOK_DEV, 0)
        slot_block = lax.dynamic_slice_in_dim(token_slot, first_row, TOK_DEV, 0)
        offset_block = lax.dynamic_slice_in_dim(offsets, first_row, TOK_DEV, 0)
        base_output = jnp.dot(normed_block, qkv_weight, preferred_element_type=jnp.float32)
        downs = adapter_down[slot_block].astype(jnp.float32)
        ranks = jnp.einsum('td,trd->tr', normed_block.astype(jnp.float32), downs).astype(jnp.bfloat16)
        ranks = lax.optimization_barrier(ranks).astype(jnp.float32)
        ups = adapter_up[slot_block].astype(jnp.float32)
        adapter_delta = jnp.einsum('tr,tro->to', ranks, ups)
        query_vectors = base_output[:, :heads_width_total] + adapter_scale_factor * adapter_delta[:, :heads_width_total]
        keys = base_output[:, heads_width_total:2 * heads_width_total]
        value_vectors = base_output[:, 2 * heads_width_total:] + adapter_scale_factor * adapter_delta[:, heads_width_total:]
        query_vectors = rotate(query_vectors.reshape(TOK_DEV, HEADS, HS), offset_block).astype(jnp.bfloat16)
        keys = rotate(keys.reshape(TOK_DEV, HEADS, HS), offset_block).astype(jnp.bfloat16)
        return (query_vectors, keys, value_vectors.reshape(TOK_DEV, HEADS, HS).astype(jnp.bfloat16))
    query_all, keys_all, values_all = lax.map(project_block, jnp.arange(block_total, dtype=jnp.int32))
    query_all = query_all.reshape(TOKENS, HEADS, HS)
    keys_all = keys_all.reshape(TOKENS, HEADS, HS)
    values_all = values_all.reshape(TOKENS, HEADS, HS)
    reach = SPAN * TOK_DEV
    keys_pad = jnp.concatenate([jnp.zeros((reach, HEADS, HS), jnp.bfloat16), keys_all], axis=0)
    values_pad = jnp.concatenate([jnp.zeros((reach, HEADS, HS), jnp.bfloat16), values_all], axis=0)
    request_pad = jnp.concatenate([jnp.full((reach,), -1, jnp.int32), global_request], axis=0)

    def attend_block(block_index):
        first_row = (block_index * TOK_DEV).astype(jnp.int32)
        query_block = lax.dynamic_slice_in_dim(query_all, first_row, TOK_DEV, 0)
        key_block = lax.dynamic_slice_in_dim(keys_pad, first_row, reach + TOK_DEV, 0)
        value_block = lax.dynamic_slice_in_dim(values_pad, first_row, reach + TOK_DEV, 0)
        key_request = lax.dynamic_slice_in_dim(request_pad, first_row, reach + TOK_DEV, 0)
        query_request = lax.dynamic_slice_in_dim(global_request, first_row, TOK_DEV, 0)
        query_index = first_row + jnp.arange(TOK_DEV, dtype=jnp.int32)
        key_index = first_row - reach + jnp.arange(reach + TOK_DEV, dtype=jnp.int32)
        allowed = (key_request[None, :] == query_request[:, None]) & (key_index[None, :] <= query_index[:, None])
        scores = jnp.einsum('qhd,khd->hqk', query_block.astype(jnp.float32), key_block.astype(jnp.float32)) * HS ** (-0.5)
        scores = jnp.where(allowed[None, :, :], scores, -1e+30)
        highest = lax.optimization_barrier(jnp.max(scores, axis=-1, keepdims=True))
        weights = jnp.exp(scores - highest)
        probs = (weights / lax.optimization_barrier(jnp.sum(weights, axis=-1, keepdims=True))).astype(jnp.bfloat16)
        attended = jnp.einsum('hqk,khd->qhd', probs.astype(jnp.float32), value_block.astype(jnp.float32))
        attended = attended.astype(jnp.bfloat16).reshape(TOK_DEV, heads_width_total)
        return jnp.dot(attended, out_weight, preferred_element_type=jnp.float32).astype(jnp.bfloat16)
    return lax.map(attend_block, jnp.arange(block_total, dtype=jnp.int32)).reshape(TOKENS, D)
```

```python
import functools

import jax
import jax.numpy as jnp
from jax import lax
from jax.experimental import pallas as pl
from jax.experimental.pallas import tpu as pltpu
from jax.sharding import PartitionSpec as P

HS = 256
SPAN = 3
MESH = pl.DeviceIdType.MESH

eps_norm = 1e-05
adapter_scale_factor = 0.5

NX, NY, NZ = 4, 4, 8


def gather_kernel(tokens, qkv, outw, down, up, wq, ws, halo, send, recv, local):
    f = lax.axis_index("fsdp")
    s = lax.axis_index("seq")
    x, c = f // 2, lax.rem(f, 2)
    y, z = s // NZ, lax.rem(s, NZ)

    def dev(dx=0, dy=0, dz=0, flip=0):
        xx = lax.rem(x + dx + NX, NX)
        yy = lax.rem(y + dy + NY, NY)
        zz = lax.rem(z + dz + NZ, NZ)
        cc = lax.rem(c + flip, 2)
        return {"fsdp": xx * 2 + cc, "seq": yy * NZ + zz}

    nxt = {"fsdp": f, "seq": lax.rem(s + 1, NY * NZ)}
    prv = {"fsdp": f, "seq": lax.rem(s + NY * NZ - 1, NY * NZ)}

    barrier = pltpu.get_barrier_semaphore()
    peers = [nxt, prv, dev(dz=1), dev(dz=-1), dev(dx=1), dev(dx=-1), dev(dy=1), dev(dy=-1), dev(flip=1)]
    for peer in peers:
        pl.semaphore_signal(barrier, inc=1, device_id=peer, device_id_type=MESH)
    pl.semaphore_wait(barrier, len(peers))

    names = {}

    def sem_of(name):
        return names.setdefault(name, len(names))

    sent = []

    def push(src, dst, name, peer):
        i = sem_of(name)
        copy = pltpu.make_async_remote_copy(
            src_ref=src, dst_ref=dst, send_sem=send.at[i], recv_sem=recv.at[i],
            device_id=peer, device_id_type=MESH,
        )
        copy.start()
        return copy

    def arrived(dst, name):
        i = sem_of(name)
        pltpu.make_async_remote_copy(
            src_ref=dst, dst_ref=dst, send_sem=send.at[i], recv_sem=recv.at[i],
            device_id=dev(), device_id_type=MESH,
        ).wait_recv()

    half = tokens.shape[0] // 2

    def rows(ref, k):
        return ref.at[pl.ds(k * half, half), :]

    for k in range(2):
        sent.append(push(rows(tokens, k), rows(halo.at[0], k), ("halo", 0, k), nxt))

    def hop(n):
        for k in range(2):
            arrived(rows(halo.at[n - 1], k), ("halo", n - 1, k))
            sent.append(push(rows(halo.at[n - 1], k), rows(halo.at[n], k), ("halo", n, k), nxt))

    def piece_q(zz):
        return wq.at[c, x, pl.ds(pl.multiple_of((y * NZ + zz) * 64, 64), 64), :]

    def piece_s(zz):
        return ws.at[c, x, :, pl.ds(pl.multiple_of((y * NZ + zz) * 32, 32), 32), :]

    cols = pl.ds(pl.multiple_of(f * 256, 256), 256)
    own = [
        pltpu.make_async_copy(qkv, piece_q(z), local.at[0]),
        pltpu.make_async_copy(outw, piece_s(z).at[0], local.at[1]),
        pltpu.make_async_copy(down.at[:, cols], piece_s(z).at[1], local.at[2]),
        pltpu.make_async_copy(up.at[:, cols], piece_s(z).at[2], local.at[3]),
    ]
    for copy in own:
        copy.start()
    for copy in own:
        copy.wait()

    for k in range(NZ - 1):
        zz = lax.rem(z + k, NZ)
        for name, piece in (("zq", piece_q), ("zs", piece_s)):
            if k > 0:
                arrived(piece(zz), (name, k - 1))
            sent.append(push(piece(zz), piece(zz), (name, k), dev(dz=-1)))
    zz = lax.rem(z + NZ - 1, NZ)
    arrived(piece_q(zz), ("zq", NZ - 2))
    arrived(piece_s(zz), ("zs", NZ - 2))

    def ring(pick, step, tag, on_ready):
        for a in range(2):
            for h, k in ((0, 1), (1, -1)):
                sent.append(push(pick(0, h, a), pick(0, h, a), (tag, "own", k, h, a), step(k)))
            for h, k in ((1, 1), (0, -1)):
                sent.append(push(pick(0, h, a), pick(0, h, a), (tag, "own", k, h, a), step(k)))
        yield
        for a in range(2):
            arrived(pick(-1, 0, a), (tag, "own", 1, 0, a))
            sent.append(push(pick(-1, 0, a), pick(-1, 0, a), (tag, "fwd", 1, a), step(1)))
            arrived(pick(1, 1, a), (tag, "own", -1, 1, a))
            sent.append(push(pick(1, 1, a), pick(1, 1, a), (tag, "fwd", -1, a), step(-1)))
            arrived(pick(-1, 1, a), (tag, "own", 1, 1, a))
            on_ready(-1, a)
            arrived(pick(1, 0, a), (tag, "own", -1, 0, a))
            on_ready(1, a)
        yield
        for a in range(2):
            arrived(pick(2, 0, a), (tag, "fwd", 1, a))
            arrived(pick(2, 1, a), (tag, "fwd", -1, a))
            on_ready(2, a)
        yield

    def nothing(d, a):
        pass

    def mid_y(d, h, a):
        yy = lax.rem(y + d + NY, NY)
        if a == 0:
            return wq.at[c, x, pl.ds(pl.multiple_of(yy * 512 + h * 256, 256), 256), :]
        return ws.at[c, x, :, pl.ds(pl.multiple_of(yy * 256 + h * 128, 128), 128), :]

    def mid_x(d, h, a):
        xx = lax.rem(x + d + NX, NX)
        if a == 0:
            return wq.at[c, xx, pl.ds(pl.multiple_of(y * 512 + h * 256, 256), 256), :]
        return ws.at[c, xx, :, pl.ds(pl.multiple_of(y * 256 + h * 128, 128), 128), :]

    def last_x(cc, d, h, a):
        xx = lax.rem(x + d + NX, NX)
        if a == 0:
            return wq.at[cc, xx, :, :] if h is None else wq.at[cc, xx, pl.ds(h * 1024, 1024), :]
        return ws.at[cc, xx, :, :, :] if h is None else ws.at[cc, xx, :, pl.ds(h * 512, 512), :]

    def last_y(cc, d, h, a):
        yy = lax.rem(y + d + NY, NY)
        if a == 0:
            base, size = (0, 512) if h is None else (h * 256, 256)
            return wq.at[cc, :, pl.ds(pl.multiple_of(yy * 512 + base, 256), size), :]
        base, size = (0, 256) if h is None else (h * 128, 128)
        return ws.at[cc, :, :, pl.ds(pl.multiple_of(yy * 256 + base, 128), size), :]

    def step_x(k):
        return dev(dx=k)

    def step_y(k):
        return dev(dy=k)

    def branch(mid, mid_step, last, last_step, other_last, cc):
        base = len(sent)
        for _ in ring(mid, mid_step, "mid", nothing):
            pass
        give = functools.partial(last, cc)

        def share(d, a):
            sent.append(push(give(d, None, a), give(d, None, a), ("core", d, a, cc), dev(flip=1)))

        steps = ring(give, last_step, "last", share)
        next(steps)
        share(0, 0)
        share(0, 1)
        hop(1)
        next(steps)
        hop(2)
        next(steps)
        for a in range(2):
            for d in (0, -1, 1, 2):
                arrived(other_last(1 - cc, d, None, a), ("core", d, a, 1 - cc))
        for k in range(2):
            arrived(rows(halo.at[2], k), ("halo", 2, k))
        for copy in sent[base:]:
            copy.wait_send()
        del sent[base:]

    @pl.when(c == 0)
    def _():
        branch(mid_y, step_y, last_x, step_x, last_y, 0)

    @pl.when(c == 1)
    def _():
        branch(mid_x, step_x, last_y, step_y, last_x, 1)

    for copy in sent:
        copy.wait_send()


def communicate(tokens, qkv_weight, out_weight, adapter_down, adapter_up):
    any_spec = pl.BlockSpec(memory_space=pl.ANY)
    bf16 = jnp.bfloat16
    return pl.pallas_call(
        gather_kernel,
        out_shape=(
            jax.ShapeDtypeStruct((2, NX, 2048, 384), bf16),
            jax.ShapeDtypeStruct((2, NX, 3, 1024, 256), bf16),
            jax.ShapeDtypeStruct((SPAN, 512, 2048), bf16),
        ),
        in_specs=[any_spec] * 5,
        out_specs=(any_spec,) * 3,
        scratch_shapes=[
            pltpu.SemaphoreType.DMA((100,)),
            pltpu.SemaphoreType.DMA((100,)),
            pltpu.SemaphoreType.DMA((4,)),
        ],
        compiler_params=pltpu.CompilerParams(collective_id=0, has_side_effects=True),
    )(tokens, qkv_weight, out_weight, adapter_down, adapter_up)


def layer_norm(token_rows):
    value_vectors = token_rows.astype(jnp.float32)
    average = jnp.mean(value_vectors, axis=-1, keepdims=True)
    centred = value_vectors - average
    variance = jnp.mean(centred * centred, axis=-1, keepdims=True)
    return (centred * lax.rsqrt(variance + eps_norm)).astype(jnp.bfloat16)


def request_info(length_row, position):
    row_ends = jnp.cumsum(length_row)
    request = jnp.sum((position[:, None] >= row_ends[None, :]).astype(jnp.int32), axis=1)
    onehot = (request[:, None] == jnp.arange(length_row.shape[0], dtype=jnp.int32)[None, :]).astype(
        jnp.int32
    )
    begins = jnp.sum(onehot * (row_ends - length_row)[None, :], axis=1)
    return (request, onehot, position - begins)


def rotate(head_rows, position):
    rotary = head_rows.shape[-1] // 4
    halfway = rotary // 2
    inverse = 10000.0 ** (-2.0 * jnp.arange(halfway, dtype=jnp.float32) / rotary)
    angles = position.astype(jnp.float32)[:, None] * inverse[None, :]
    cosine = jnp.cos(angles)[:, None, :]
    sine_part = jnp.sin(angles)[:, None, :]
    leading = head_rows[..., :halfway]
    trailing = head_rows[..., halfway:rotary]
    return jnp.concatenate(
        [
            leading * cosine - trailing * sine_part,
            trailing * cosine + leading * sine_part,
            head_rows[..., rotary:],
        ],
        axis=-1,
    )


def per_device(
    tokens, qkv_weight, out_weight, adapter_down, adapter_up, lengths, adapter_ids, adapter_slot
):
    count = tokens.shape[0]
    group_index = lax.axis_index("fsdp")
    block_index = lax.axis_index("seq")
    wq, ws, halo = communicate(
        tokens, qkv_weight, out_weight, adapter_down.reshape(32, 2048), adapter_up.reshape(32, 2048)
    )
    qkv_full = wq.transpose(2, 1, 0, 3).reshape(2048, 3072)
    small = ws.transpose(2, 3, 1, 0, 4).reshape(3, 1024, 2048)
    out_full = small[0]
    downs = small[1].reshape(64, 16, 2048)
    ups = small[2].reshape(64, 16, 2048)
    length_row = lax.dynamic_index_in_dim(lengths, group_index, 0, keepdims=False)
    ids_row = lax.dynamic_index_in_dim(adapter_ids, group_index, 0, keepdims=False)
    request_slot = adapter_slot[ids_row]
    picked_down = downs[request_slot]
    picked_up = ups[request_slot]
    window = jnp.concatenate([tokens[None], halo], axis=0).reshape(4 * count, 2048)
    depth = 4
    key_position = (
        (block_index - jnp.arange(depth, dtype=jnp.int32))[:, None] * count
        + jnp.arange(count, dtype=jnp.int32)[None, :]
    ).reshape(-1)
    key_request, key_onehot, key_offsets = request_info(length_row, key_position)
    position, request, offsets = key_position[:count], key_request[:count], key_offsets[:count]
    normed = layer_norm(window)
    ranks = jnp.einsum("td,ard->tar", normed, picked_down, preferred_element_type=jnp.float32)
    ranks = jnp.where(key_onehot[:, :, None] > 0, ranks, 0.0).astype(jnp.bfloat16)
    ranks = ranks.reshape(depth * count, 256)
    up_flat = picked_up.reshape(256, 2048)
    width = 1024
    query = jnp.dot(normed[:count], qkv_full[:, :width], preferred_element_type=jnp.float32)
    query = query + adapter_scale_factor * jnp.dot(
        ranks[:count], up_flat[:, :width], preferred_element_type=jnp.float32
    )
    keys = jnp.dot(normed, qkv_full[:, width : 2 * width], preferred_element_type=jnp.float32)
    values = jnp.dot(normed, qkv_full[:, 2 * width :], preferred_element_type=jnp.float32)
    values = values + adapter_scale_factor * jnp.dot(
        ranks, up_flat[:, width:], preferred_element_type=jnp.float32
    )
    query = rotate(query.reshape(count, 4, HS), offsets).astype(jnp.bfloat16)
    keys = rotate(keys.reshape(depth * count, 4, HS), key_offsets).astype(jnp.bfloat16)
    values = values.astype(jnp.bfloat16).reshape(depth * count, 4, HS)
    allowed = (
        (key_request[None, :] == request[:, None])
        & (key_position[None, :] >= 0)
        & (key_position[None, :] <= position[:, None])
    )
    scores = jnp.einsum("qhd,khd->hqk", query, keys, preferred_element_type=jnp.float32) * HS ** (-0.5)
    scores = jnp.where(allowed[None, :, :], scores, -1e30)
    highest = jnp.max(scores, axis=-1, keepdims=True)
    weights = jnp.exp(scores - highest)
    probs = (weights / jnp.sum(weights, axis=-1, keepdims=True)).astype(jnp.bfloat16)
    attended = jnp.einsum("hqk,khd->qhd", probs, values, preferred_element_type=jnp.float32)
    attended = attended.astype(jnp.bfloat16).reshape(count, width)
    mixed = jnp.dot(attended, out_full, preferred_element_type=jnp.float32)
    return mixed.astype(jnp.bfloat16)


def solution(mesh):
    in_specs = (
        P(("fsdp", "seq"), None),
        P("seq", "fsdp"),
        P("seq", "fsdp"),
        P("seq", None, None),
        P("seq", None, None),
        P(),
        P(),
        P(),
    )
    out_specs = P(("fsdp", "seq"), None)
    return jax.shard_map(
        per_device, mesh=mesh, in_specs=in_specs, out_specs=out_specs, check_vma=False
    )
```

```python
import functools

import jax
import jax.numpy as jnp
import numpy as np
from jax import lax
from jax.experimental import pallas as pl
from jax.experimental.pallas import tpu as pltpu
from jax.sharding import PartitionSpec as P

HS = 256
HEADS = 4
SPAN = 3
TOK = 512
REQS = 16
WIDTH = 1024
NX, NY, NZ = 4, 4, 8
MESH = pl.DeviceIdType.MESH
bf16, f32, i32 = jnp.bfloat16, jnp.float32, jnp.int32

eps_norm = 1e-05
adapter_scale_factor = 0.5


def whole_kernel(
    lengths, ids, slots, inverse, tokens, qkv, outw, down, up,
    out,
    wq, ws, H, stage, kbuf, vbuf, qbuf, onehot, dsel, usel, rbuf, acc, mbuf, lbuf, ctab, stab, begins, owner, bias, obuf,
    send, recv, local, osem,
):
    f = lax.axis_index("fsdp")
    s = lax.axis_index("seq")
    x, c = f // 2, lax.rem(f, 2)
    y, z = s // NZ, lax.rem(s, NZ)
    xs = {d: lax.rem(x + d + NX, NX) for d in (-1, 0, 1, 2)}
    ys = {d: lax.rem(y + d + NY, NY) for d in (-1, 0, 1, 2)}
    zs = {d: lax.rem(z + d, NZ) for d in range(NZ)}
    at = pl.multiple_of
    dev_x = {d: {"fsdp": xs[d] * 2 + c, "seq": s} for d in (1, -1)}
    dev_y = {d: {"fsdp": f, "seq": ys[d] * NZ + z} for d in (1, -1)}
    dev_z = {d: {"fsdp": f, "seq": y * NZ + zs[d % NZ]} for d in (1, -1)}
    dev_c = {"fsdp": x * 2 + (1 - c), "seq": s}
    self_id = {"fsdp": f, "seq": s}

    q_piece = {d: at((y * NZ + zs[d]) * 64, 64) for d in range(NZ)}
    s_piece = {d: at((y * NZ + zs[d]) * 32, 32) for d in range(NZ)}
    q_rows = {d: {h: at(ys[d] * 512 + o, 256) for h, o in ((None, 0), (0, 0), (1, 256))} for d in ys}
    s_rows = {d: {h: at(ys[d] * 256 + o, 128) for h, o in ((None, 0), (0, 0), (1, 128))} for d in ys}
    cols = pl.ds(at(f * 256, 256), 256)

    load = pltpu.make_async_copy(tokens, H.at[0], local.at[4])
    load.start()

    def piece_q(d):
        return wq.at[c, x, :, pl.ds(q_piece[d], 64), :]

    def piece_s(d):
        return ws.at[c, x, :, pl.ds(s_piece[d], 32), :]

    own = [
        pltpu.make_async_copy(outw, piece_s(0).at[0], local.at[0]),
        pltpu.make_async_copy(down.at[:, cols], piece_s(0).at[1], local.at[1]),
        pltpu.make_async_copy(up.at[:, cols], piece_s(0).at[2], local.at[2]),
    ] + [
        pltpu.make_async_copy(qkv.at[:, pl.ds(t * 128, 128)], piece_q(0).at[t], local.at[5 + t])
        for t in range(3)
    ]
    for copy in own:
        copy.start()

    barrier = pltpu.get_barrier_semaphore()
    peers = [dev_x[1], dev_x[-1], dev_y[1], dev_y[-1], dev_z[1], dev_z[-1], dev_c]
    for peer in peers:
        pl.semaphore_signal(barrier, inc=1, device_id=peer, device_id_type=MESH)
    pl.semaphore_wait(barrier, len(peers))

    names = {}

    def sem_of(name):
        return names.setdefault(name, len(names))

    def push(src, dst, name, peer, recv_name=None):
        copy = pltpu.make_async_remote_copy(
            src_ref=src, dst_ref=dst,
            send_sem=send.at[sem_of(name)], recv_sem=recv.at[sem_of(recv_name or name)],
            device_id=peer, device_id_type=MESH,
        )
        copy.start()
        return copy

    def arrived(dst, name):
        i = sem_of(name)
        pltpu.make_async_remote_copy(
            src_ref=dst, dst_ref=dst, send_sem=send.at[i], recv_sem=recv.at[i],
            device_id=self_id, device_id_type=MESH,
        ).wait_recv()

    def departed(src, name):
        i = sem_of(name)
        pltpu.make_async_remote_copy(
            src_ref=src, dst_ref=src, send_sem=send.at[i], recv_sem=recv.at[i],
            device_id=self_id, device_id_type=MESH,
        ).wait_send()

    half = TOK // 2

    def part(n, k):
        return H.at[n, pl.ds(k * half, half), :]

    def hop_part(n, k):
        @pl.when(z != NZ - 1)
        def _():
            push(part(n, k), part(n + 1, k), ("halo", n, k), dev_z[1])

        @pl.when(z == NZ - 1)
        def _():
            push(part(n, k), stage.at[n], ("halo", n, k), dev_z[1] if k == 0 else dev_y[1], ("stage", n))

    def hop(n):
        for k in range(2):
            arrived(part(n, k), ("halo", n - 1, k))
            hop_part(n, k)

    def relay(n):
        @pl.when(z == 0)
        def _():
            arrived(stage.at[n], ("stage", n))
            push(stage.at[n], part(n + 1, 0), ("relay", n), dev_y[1], ("halo", n, 0))

        @pl.when(z == NZ - 1)
        def _():
            arrived(stage.at[n], ("stage", n))
            push(stage.at[n], part(n + 1, 1), ("relay", n), dev_z[1], ("halo", n, 1))

    load.wait()
    for k in range(2):
        @pl.loop(0, half // 32)
        def _(i):
            r = pl.ds(at(k * half + i * 32, 32), 32)
            v = H[0, r, :].astype(f32)
            mean = jnp.mean(v, axis=-1, keepdims=True)
            centred = v - mean
            variance = jnp.mean(centred * centred, axis=-1, keepdims=True)
            H[0, r, :] = (centred * lax.rsqrt(variance + eps_norm)).astype(bf16)

        hop_part(0, k)

    for copy in own:
        copy.wait()

    for k in range(NZ - 1):
        for name, piece in (("zq", piece_q), ("zs", piece_s)):
            if k > 0:
                arrived(piece(k), (name, k - 1))
            push(piece(k), piece(k), (name, k), dev_z[-1])

    def end_z(name, piece):
        arrived(piece(NZ - 1), (name, NZ - 2))

    def rows_of(table, base, size):
        return pl.ds(base, size)

    def mid_y(d, h, a):
        if a == 0:
            return wq.at[c, x, :, pl.ds(q_rows[d][h], 256), :]
        return ws.at[c, x, :, pl.ds(s_rows[d][h], 128), :]

    def mid_x(d, h, a):
        if a == 0:
            return wq.at[c, xs[d], :, pl.ds(q_rows[0][h], 256), :]
        return ws.at[c, xs[d], :, pl.ds(s_rows[0][h], 128), :]

    def last_x(cc, d, h, a):
        if a == 0:
            return wq.at[cc, xs[d]] if h is None else wq.at[cc, xs[d], :, pl.ds(h * 1024, 1024), :]
        return ws.at[cc, xs[d]] if h is None else ws.at[cc, xs[d], :, pl.ds(h * 512, 512), :]

    def last_y(cc, d, h, a):
        if a == 0:
            return wq.at[cc, :, :, pl.ds(q_rows[d][h], 512 if h is None else 256), :]
        return ws.at[cc, :, :, pl.ds(s_rows[d][h], 256 if h is None else 128), :]

    class Ring:
        def __init__(self, pick, devs, tag):
            self.pick, self.devs, self.tag = pick, devs, tag

        def begin(self, a):
            for h, k in ((0, 1), (1, -1), (1, 1), (0, -1)):
                push(self.pick(0, h, a), self.pick(0, h, a), (self.tag, "own", k, h, a), self.devs[k])

        def forward(self, a):
            for k, h in ((1, 0), (-1, 1)):
                arrived(self.pick(-k, h, a), (self.tag, "own", k, h, a))
                push(self.pick(-k, h, a), self.pick(-k, h, a), (self.tag, "fwd", k, a), self.devs[k])

        def near(self, a):
            for k, h in ((1, 1), (-1, 0)):
                arrived(self.pick(-k, h, a), (self.tag, "own", k, h, a))

        def far(self, a):
            for k, h in ((1, 0), (-1, 1)):
                arrived(self.pick(2, h, a), (self.tag, "fwd", k, a))

        def drain(self):
            for a in range(2):
                for h, k in ((0, 1), (1, -1), (1, 1), (0, -1)):
                    departed(self.pick(0, h, a), (self.tag, "own", k, h, a))
                for k, h in ((1, 0), (-1, 1)):
                    departed(self.pick(-k, h, a), (self.tag, "fwd", k, a))

    plans = []
    for cc, mid, mid_devs, last, last_devs, other in (
        (0, mid_y, dev_y, last_x, dev_x, last_y),
        (1, mid_x, dev_x, last_y, dev_y, last_x),
    ):
        plans.append((
            Ring(mid, mid_devs, "mid"),
            Ring(functools.partial(last, cc), last_devs, "last"),
            functools.partial(last, cc),
            functools.partial(other, 1 - cc),
            cc,
        ))

    def per_core(body):
        for plan in plans:
            @pl.when(c == plan[4])
            def _():
                body(*plan)

    def share(give, cc, a, *ds):
        for d in ds:
            push(give(d, None, a), give(d, None, a), ("core", d, a, cc), dev_c)

    def first(mid, last, give, take, cc):
        end_z("zq", piece_q)
        mid.begin(0)
        end_z("zs", piece_s)
        mid.forward(0)
        mid.begin(1)
        mid.near(0)
        mid.far(0)
        last.begin(0)
        share(give, cc, 0, 0)
        mid.forward(1)
        mid.near(1)
        mid.far(1)

    def second(mid, last, give, take, cc):
        last.forward(0)
        last.begin(1)
        share(give, cc, 1, 0)
        last.near(0)
        share(give, cc, 0, -1, 1)

    def third(mid, last, give, take, cc):
        last.far(0)
        share(give, cc, 0, 2)
        last.forward(1)
        last.near(1)
        share(give, cc, 1, -1, 1)

    def fourth(mid, last, give, take, cc):
        last.far(1)
        share(give, cc, 1, 2)

    def fifth(mid, last, give, take, cc):
        for a in range(2):
            for d in (0, -1, 1, 2):
                arrived(take(d, None, a), ("core", d, a, 1 - cc))

    def drain(mid, last, give, take, cc):
        mid.drain()
        last.drain()
        for a in range(2):
            for d in (0, -1, 1, 2):
                departed(give(d, None, a), ("core", d, a, cc))

    per_core(first)
    relay(0)

    lane = lax.broadcasted_iota(i32, (TOK, 128), 1)
    token = lax.broadcasted_iota(i32, (TOK, 128), 0)

    @pl.loop(0, SPAN + 1)
    def _(j):
        position = (s - j) * TOK + token
        ends = jnp.int32(0)
        begin = jnp.zeros((TOK, 128), i32)
        request = jnp.zeros((TOK, 128), i32)
        for r in range(REQS - 1):
            ends = ends + lengths[f, r]
            past = position >= ends
            begin = jnp.where(past, ends, begin)
            request = request + past.astype(i32)
        begins[j] = begin
        owner[j] = request
        angle = (position - begin).astype(f32) * inverse[0:1, :]
        ctab[j] = jnp.where(lane < 64, jnp.cos(angle), 1.0)
        sine = jnp.sin(angle)
        stab[j] = jnp.where(lane < 32, -sine, jnp.where(lane < 64, sine, 0.0))

    per_core(second)
    hop(1)
    per_core(third)
    relay(1)
    per_core(fourth)
    hop(2)
    per_core(fifth)

    table = slots[...].astype(f32)
    at_slot = lax.broadcasted_iota(i32, (1, 64), 1)
    inner = lax.broadcasted_iota(i32, (16, 1024), 0)
    column = lax.broadcasted_iota(i32, (16, 1024), 1)
    for r in range(REQS):
        slot = jnp.sum(jnp.where(at_slot == ids[f, r], table, 0.0), axis=-1, keepdims=True)
        hit = column == slot.astype(i32) * 16 + inner
        onehot[r * 16 : (r + 1) * 16, :] = jnp.where(hit, 1.0, 0.0).astype(bf16)

    for g in range(8):
        for n, picked in ((1, dsel), (2, usel)):
            picked[:, g * 256 : (g + 1) * 256] = jnp.dot(
                onehot[...], ws[g % 2, g // 2, n], preferred_element_type=f32
            ).astype(bf16)

    def weight(tile):
        g = tile // 3
        return wq[lax.rem(g, 2), g // 2, lax.rem(tile, 3)]

    def columns(head):
        return jnp.concatenate([weight(2 * head), weight(2 * head + 1)], axis=1)

    def dot(a, b):
        return jnp.dot(a, b, preferred_element_type=f32)

    def rotated(v, j):
        first_half = v[:, :128]
        swapped = jnp.where(
            lane < 32, pltpu.roll(first_half, 96, 1), pltpu.roll(first_half, 32, 1)
        )
        return jnp.concatenate([first_half * ctab[j] + swapped * stab[j], v[:, 128:]], axis=1)

    def ranks(j):
        r = lax.dot_general(H[j], dsel[...], (((1,), (1,)), ((), ())), preferred_element_type=f32)
        column = lax.broadcasted_iota(i32, (TOK, 256), 1) // 16
        request = jnp.concatenate([owner[j]] * 2, axis=1)
        rbuf[...] = jnp.where(column == request, r, 0.0).astype(bf16)

    def scatter_bias(j):
        begin = jnp.concatenate([begins[0]] * 4, axis=1)
        row = lax.broadcasted_iota(i32, (TOK, TOK), 0) + s * TOK
        col = lax.broadcasted_iota(i32, (TOK, TOK), 1) + (s - j) * TOK
        bias[...] = jnp.where((col >= begin) & (col <= row), 0.0, -1e30).astype(f32)

    def block(j):
        ranks(j)
        scatter_bias(j)

        @pl.loop(0, HEADS)
        def _(h):
            u = usel[:, pl.ds(at(h * HS + WIDTH, HS), HS)]
            kbuf[...] = rotated(dot(H[j], columns(HEADS + h)), j).astype(bf16)
            value = dot(H[j], columns(2 * HEADS + h)) + adapter_scale_factor * dot(rbuf[...], u)
            vbuf[...] = value.astype(bf16)
            if j == 0:
                uq = usel[:, pl.ds(at(h * HS, HS), HS)]
                q = dot(H[0], columns(h)) + adapter_scale_factor * dot(rbuf[...], uq)
                qbuf[h] = rotated(q, 0).astype(bf16) * jnp.asarray(HS ** (-0.5), bf16)

            @pl.loop(0, 2)
            def _(i):
                r = pl.ds(at(i * 256, 256), 256)
                scores = lax.dot_general(
                    qbuf[h, r, :], kbuf[...], (((1,), (1,)), ((), ())), preferred_element_type=f32
                ) + bias[r, :]
                top = jnp.max(scores, axis=-1, keepdims=True)
                if j == 0:
                    p = jnp.exp(scores - top)
                    total = jnp.sum(p, axis=-1, keepdims=True)
                    acc[h, r, :] = dot(p.astype(bf16), vbuf[...])
                else:
                    before = mbuf[h, r, :][:, :1]
                    top = jnp.maximum(top, before)
                    fade = jnp.exp(before - top)
                    p = jnp.exp(scores - top)
                    total = fade * lbuf[h, r, :][:, :1] + jnp.sum(p, axis=-1, keepdims=True)
                    acc[h, r, :] = fade * acc[h, r, :] + dot(p.astype(bf16), vbuf[...])
                if j == SPAN:
                    qbuf[h, r, :] = (acc[h, r, :] / total).astype(bf16)
                else:
                    mbuf[h, r, :] = jnp.broadcast_to(top, (256, 128))
                    lbuf[h, r, :] = jnp.broadcast_to(total, (256, 128))

    block(0)
    block(1)
    relay(2)
    block(2)
    for k in range(2):
        arrived(part(3, k), ("halo", 2, k))
    block(3)

    for g in range(8):
        if g >= 2:
            pltpu.make_async_copy(obuf.at[g % 2], out.at[:, pl.ds((g - 2) * 256, 256)], osem.at[g % 2]).wait()
        attended = jnp.concatenate([qbuf[h] for h in range(HEADS)], axis=1)
        obuf[g % 2] = dot(attended, ws[g % 2, g // 2, 0]).astype(bf16)
        pltpu.make_async_copy(obuf.at[g % 2], out.at[:, pl.ds(g * 256, 256)], osem.at[g % 2]).start()
    for g in (6, 7):
        pltpu.make_async_copy(obuf.at[g % 2], out.at[:, pl.ds(g * 256, 256)], osem.at[g % 2]).wait()

    for n in range(SPAN):
        for k in range(2):
            departed(part(n, k), ("halo", n, k))

        @pl.when((z == 0) | (z == NZ - 1))
        def _():
            departed(stage.at[n], ("relay", n))
    for k in range(NZ - 1):
        departed(piece_q(k), ("zq", k))
        departed(piece_s(k), ("zs", k))
    per_core(drain)


def run_whole(lengths, ids, slots, inverse, tokens, qkv_weight, out_weight, down, up):
    anywhere = pl.BlockSpec(memory_space=pl.ANY)
    scalar = pl.BlockSpec(memory_space=pltpu.SMEM)
    return pl.pallas_call(
        whole_kernel,
        out_shape=jax.ShapeDtypeStruct((TOK, 2 * WIDTH), bf16),
        in_specs=[scalar] * 2 + [pl.BlockSpec(memory_space=pltpu.VMEM)] * 2 + [anywhere] * 5,
        out_specs=anywhere,
        scratch_shapes=[
            pltpu.VMEM((2, NX, 3, 2048, 128), bf16),
            pltpu.VMEM((2, NX, 3, 1024, 256), bf16),
            pltpu.VMEM((SPAN + 1, TOK, 2048), bf16),
            pltpu.VMEM((SPAN, TOK // 2, 2048), bf16),
            pltpu.VMEM((TOK, HS), bf16),
            pltpu.VMEM((TOK, HS), bf16),
            pltpu.VMEM((HEADS, TOK, HS), bf16),
            pltpu.VMEM((256, 1024), bf16),
            pltpu.VMEM((256, 2048), bf16),
            pltpu.VMEM((256, 2048), bf16),
            pltpu.VMEM((TOK, 256), bf16),
            pltpu.VMEM((HEADS, TOK, HS), f32),
            pltpu.VMEM((HEADS, TOK, 128), f32),
            pltpu.VMEM((HEADS, TOK, 128), f32),
            pltpu.VMEM((SPAN + 1, TOK, 128), f32),
            pltpu.VMEM((SPAN + 1, TOK, 128), f32),
            pltpu.VMEM((SPAN + 1, TOK, 128), i32),
            pltpu.VMEM((SPAN + 1, TOK, 128), i32),
            pltpu.VMEM((TOK, TOK), f32),
            pltpu.VMEM((2, TOK, 256), bf16),
            pltpu.SemaphoreType.DMA((110,)),
            pltpu.SemaphoreType.DMA((110,)),
            pltpu.SemaphoreType.DMA((8,)),
            pltpu.SemaphoreType.DMA((2,)),
        ],
        compiler_params=pltpu.CompilerParams(
            collective_id=0, has_side_effects=True, vmem_limit_bytes=62 * 1024 * 1024
        ),
    )(lengths, ids, slots, inverse, tokens, qkv_weight, out_weight, down, up)


def per_device(
    tokens, qkv_weight, out_weight, adapter_down, adapter_up, lengths, adapter_ids, adapter_slot
):
    rotary = HS // 4
    inverse = 10000.0 ** (-2.0 * (np.arange(128) % (rotary // 2)) / rotary)
    inverse = jnp.asarray(np.tile(inverse[None, :], (8, 1)), f32)
    return run_whole(
        lengths, adapter_ids, adapter_slot.reshape(1, -1), inverse, tokens, qkv_weight, out_weight,
        adapter_down.reshape(-1, 2048), adapter_up.reshape(-1, 2048),
    )


def solution(mesh):
    in_specs = (
        P(("fsdp", "seq"), None),
        P("seq", "fsdp"),
        P("seq", "fsdp"),
        P("seq", None, None),
        P("seq", None, None),
        P(),
        P(),
        P(),
    )
    out_specs = P(("fsdp", "seq"), None)
    return jax.shard_map(
        per_device, mesh=mesh, in_specs=in_specs, out_specs=out_specs, check_vma=False
    )
```

```python
import functools

import jax
import jax.numpy as jnp
import numpy as np
from jax import lax
from jax.experimental import pallas as pl
from jax.experimental.pallas import tpu as pltpu
from jax.sharding import PartitionSpec as P

HS = 256
HEADS = 4
SPAN = 3
TOK = 512
REQS = 16
WIDTH = 1024
NX, NY, NZ = 4, 4, 8
MESH = pl.DeviceIdType.MESH
HEADS_AT_ONCE = 1
DETOUR = True
bf16, f32, i32 = jnp.bfloat16, jnp.float32, jnp.int32

eps_norm = 1e-05
adapter_scale_factor = 0.5


def whole_kernel(
    lengths, ids, slots, inverse, tokens, qkv, outw, down, up,
    out,
    wq, ws, H, kbuf, vbuf, qbuf, onehot, dsel, usel, rbuf, acc, vpre, mbuf, lbuf, ctab, stab, begins, owner, bias, obuf, att,
    send, recv, local, osem,
):
    f = lax.axis_index("fsdp")
    s = lax.axis_index("seq")
    x, c = f // 2, lax.rem(f, 2)
    y, z = s // NZ, lax.rem(s, NZ)
    xs = {d: lax.rem(x + d + NX, NX) for d in (-1, 0, 1, 2)}
    ys = {d: lax.rem(y + d + NY, NY) for d in (-1, 0, 1, 2)}
    zs = {d: lax.rem(z + d, NZ) for d in range(NZ)}
    at = pl.multiple_of
    dev_x = {d: {"fsdp": xs[d] * 2 + c, "seq": s} for d in (1, -1)}
    dev_y = {d: {"fsdp": f, "seq": ys[d] * NZ + z} for d in (1, -1)}
    dev_z = {d: {"fsdp": f, "seq": y * NZ + zs[d % NZ]} for d in (1, -1)}
    dev_c = {"fsdp": x * 2 + (1 - c), "seq": s}
    self_id = {"fsdp": f, "seq": s}

    q_piece = {d: at((y * NZ + zs[d]) * 64, 64) for d in range(NZ)}
    s_piece = {d: at((y * NZ + zs[d]) * 32, 32) for d in range(NZ)}
    q_rows = {d: {h: at(ys[d] * 512 + o, 256) for h, o in ((None, 0), (0, 0), (1, 256))} for d in ys}
    s_rows = {d: {h: at(ys[d] * 256 + o, 128) for h, o in ((None, 0), (0, 0), (1, 128))} for d in ys}
    cols = pl.ds(at(f * 256, 256), 256)

    load = pltpu.make_async_copy(tokens, H.at[0], local.at[4])
    load.start()

    def piece_q(d):
        return wq.at[c, x, :, pl.ds(q_piece[d], 64), :]

    def piece_s(d):
        return ws.at[c, x, :, pl.ds(s_piece[d], 32), :]

    own = [
        pltpu.make_async_copy(outw, piece_s(0).at[0], local.at[0]),
        pltpu.make_async_copy(down.at[:, cols], piece_s(0).at[1], local.at[1]),
        pltpu.make_async_copy(up.at[:, cols], piece_s(0).at[2], local.at[2]),
    ] + [
        pltpu.make_async_copy(qkv.at[:, pl.ds(t * 128, 128)], piece_q(0).at[t], local.at[5 + t])
        for t in range(3)
    ]
    for copy in own:
        copy.start()

    barrier = pltpu.get_barrier_semaphore()
    total = NY * NZ
    following = {"fsdp": f, "seq": lax.rem(s + 1, total)}
    preceding = {"fsdp": f, "seq": lax.rem(s + total - 1, total)}
    peers = [following, preceding, dev_x[1], dev_x[-1], dev_y[1], dev_y[-1], dev_z[1], dev_z[-1], dev_c]
    for peer in peers:
        pl.semaphore_signal(barrier, inc=1, device_id=peer, device_id_type=MESH)
    pl.semaphore_wait(barrier, len(peers))

    names = {}

    def sem_of(name):
        return names.setdefault(name, len(names))

    def push(src, dst, name, peer, recv_name=None):
        copy = pltpu.make_async_remote_copy(
            src_ref=src, dst_ref=dst,
            send_sem=send.at[sem_of(name)], recv_sem=recv.at[sem_of(recv_name or name)],
            device_id=peer, device_id_type=MESH,
        )
        copy.start()
        return copy

    def arrived(dst, name):
        i = sem_of(name)
        pltpu.make_async_remote_copy(
            src_ref=dst, dst_ref=dst, send_sem=send.at[i], recv_sem=recv.at[i],
            device_id=self_id, device_id_type=MESH,
        ).wait_recv()

    def departed(src, name):
        i = sem_of(name)
        pltpu.make_async_remote_copy(
            src_ref=src, dst_ref=src, send_sem=send.at[i], recv_sem=recv.at[i],
            device_id=self_id, device_id_type=MESH,
        ).wait_send()

    half = TOK // 2

    def part(n, k):
        return H.at[n, pl.ds(k * half, half), :]

    def hop_part(n, k):
        push(part(n, k), part(n + 1, k), ("halo", n, k), following)

    def hop(n):
        for k in range(2):
            arrived(part(n, k), ("halo", n - 1, k))
            hop_part(n, k)

    lane = lax.broadcasted_iota(i32, (TOK, 128), 1)
    token = lax.broadcasted_iota(i32, (TOK, 128), 0)

    def norm(k):
        @pl.loop(0, half // 64)
        def _(i):
            r = pl.ds(at(k * half + i * 64, 64), 64)
            v = H[0, r, :].astype(f32)
            mean = jnp.mean(v, axis=-1, keepdims=True)
            centred = v - mean
            variance = jnp.mean(centred * centred, axis=-1, keepdims=True)
            H[0, r, :] = (centred * lax.rsqrt(variance + eps_norm)).astype(bf16)

    def tables(j):
        position = (s - j) * TOK + token
        ends = jnp.int32(0)
        begin = jnp.zeros((TOK, 128), i32)
        request = jnp.zeros((TOK, 128), i32)
        for r in range(REQS - 1):
            ends = ends + lengths[f, r]
            past = position >= ends
            begin = jnp.where(past, ends, begin)
            request = request + past.astype(i32)
        if j == 0:
            begins[...] = begin
        owner[j] = request
        angle = (position - begin).astype(f32) * inverse[0:1, :]
        ctab[j] = jnp.where(lane < 64, jnp.cos(angle), 1.0)
        sine = jnp.sin(angle)
        stab[j] = jnp.where(lane < 32, -sine, jnp.where(lane < 64, sine, 0.0))

    def z_step(k):
        for name, piece in (("zq", piece_q), ("zs", piece_s)):
            if k > 0:
                arrived(piece(k), (name, k - 1))
            push(piece(k), piece(k), (name, k), dev_z[-1])

    load.wait()
    norm(0)
    hop_part(0, 0)
    for copy in own:
        copy.wait()
    z_step(0)
    norm(1)
    hop_part(0, 1)
    z_step(1)
    for k in range(2, NZ - 1):
        z_step(k)
        if k - 2 <= SPAN:
            tables(k - 2)

    def end_z(name, piece):
        arrived(piece(NZ - 1), (name, NZ - 2))

    def mid_y(d, h, a):
        if a == 0:
            return wq.at[c, x, :, pl.ds(q_rows[d][h], 256), :]
        return ws.at[c, x, :, pl.ds(s_rows[d][h], 128), :]

    def mid_x(d, h, a):
        if a == 0:
            return wq.at[c, xs[d], :, pl.ds(q_rows[0][h], 256), :]
        return ws.at[c, xs[d], :, pl.ds(s_rows[0][h], 128), :]

    def last_x(cc, d, h, a):
        if a == 0:
            return wq.at[cc, xs[d]] if h is None else wq.at[cc, xs[d], :, pl.ds(h * 1024, 1024), :]
        return ws.at[cc, xs[d]] if h is None else ws.at[cc, xs[d], :, pl.ds(h * 512, 512), :]

    def last_y(cc, d, h, a):
        if a == 0:
            return wq.at[cc, :, :, pl.ds(q_rows[d][h], 512 if h is None else 256), :]
        return ws.at[cc, :, :, pl.ds(s_rows[d][h], 256 if h is None else 128), :]

    inner_plane = z != 0

    class Ring:
        def __init__(self, pick, devs, tag, detour=False):
            self.pick, self.devs, self.tag, self.detour = pick, devs, tag, detour

        def send(self, d, h, a, name, k):
            if self.detour and k == 1:
                @pl.when(inner_plane)
                def _():
                    push(self.pick(d, h, a), self.pick(d, h, a), name, self.devs[k])
            else:
                push(self.pick(d, h, a), self.pick(d, h, a), name, self.devs[k])

        def get(self, d, h, a, name, k):
            arrived(self.pick(d, h, a), name)
            if self.detour and k == 1:
                @pl.when(z == 1)
                def _():
                    push(self.pick(d, h, a), self.pick(d, h, a), ("detour",) + name, dev_z[-1], name)

        def begin(self, a):
            for h, k in ((0, 1), (1, -1), (1, 1), (0, -1)):
                self.send(0, h, a, (self.tag, "own", k, h, a), k)

        def forward(self, a):
            for k, h in ((1, 0), (-1, 1)):
                self.get(-k, h, a, (self.tag, "own", k, h, a), k)
                self.send(-k, h, a, (self.tag, "fwd", k, a), k)

        def near(self, a):
            for k, h in ((1, 1), (-1, 0)):
                self.get(-k, h, a, (self.tag, "own", k, h, a), k)

        def far(self, a):
            for k, h in ((1, 0), (-1, 1)):
                self.get(2, h, a, (self.tag, "fwd", k, a), k)

        def left(self, d, h, a, name, k):
            if self.detour and k == 1:
                @pl.when(inner_plane)
                def _():
                    departed(self.pick(d, h, a), name)
            else:
                departed(self.pick(d, h, a), name)

        def drain(self):
            for a in range(2):
                for h, k in ((0, 1), (1, -1), (1, 1), (0, -1)):
                    self.left(0, h, a, (self.tag, "own", k, h, a), k)
                for k, h in ((1, 0), (-1, 1)):
                    self.left(-k, h, a, (self.tag, "fwd", k, a), k)
                if self.detour:
                    @pl.when(z == 1)
                    def _():
                        for d, h, name in (
                            (-1, 0, (self.tag, "own", 1, 0, a)),
                            (-1, 1, (self.tag, "own", 1, 1, a)),
                            (2, 0, (self.tag, "fwd", 1, a)),
                        ):
                            departed(self.pick(d, h, a), ("detour",) + name)

    plans = []
    for cc, mid, mid_devs, last, last_devs, other in (
        (0, mid_y, dev_y, last_x, dev_x, last_y),
        (1, mid_x, dev_x, last_y, dev_y, last_x),
    ):
        plans.append((
            Ring(mid, mid_devs, "mid", detour=DETOUR and cc == 0),
            Ring(functools.partial(last, cc), last_devs, "last", detour=DETOUR and cc == 1),
            functools.partial(last, cc),
            functools.partial(other, 1 - cc),
            cc,
        ))

    def per_core(body):
        for plan in plans:
            @pl.when(c == plan[4])
            def _():
                body(*plan)

    def share(give, cc, a, *ds):
        for d in ds:
            push(give(d, None, a), give(d, None, a), ("core", d, a, cc), dev_c)

    def first(mid, last, give, take, cc):
        end_z("zq", piece_q)
        mid.begin(0)
        end_z("zs", piece_s)
        mid.forward(0)
        mid.begin(1)
        mid.near(0)
        mid.far(0)
        last.begin(0)
        share(give, cc, 0, 0)

    def first_rest(mid, last, give, take, cc):
        mid.forward(1)
        mid.near(1)
        mid.far(1)
        last.forward(0)
        last.begin(1)
        share(give, cc, 1, 0)

    def second(mid, last, give, take, cc):
        last.near(0)
        share(give, cc, 0, -1, 1)
        last.far(0)
        share(give, cc, 0, 2)
        for d in (0, -1, 1, 2):
            arrived(take(d, None, 0), ("core", d, 0, 1 - cc))

    def third(mid, last, give, take, cc):
        last.forward(1)

    def fourth(mid, last, give, take, cc):
        last.near(1)
        share(give, cc, 1, -1, 1)

    def fifth(mid, last, give, take, cc):
        last.far(1)
        share(give, cc, 1, 2)
        for d in (0, -1, 1, 2):
            arrived(take(d, None, 1), ("core", d, 1, 1 - cc))

    def drain(mid, last, give, take, cc):
        mid.drain()
        last.drain()
        for a in range(2):
            for d in (0, -1, 1, 2):
                departed(give(d, None, a), ("core", d, a, cc))

    def weight(tile):
        g = tile // 3
        return wq[lax.rem(g, 2), g // 2, lax.rem(tile, 3)]

    def columns(head):
        return jnp.concatenate([weight(2 * head), weight(2 * head + 1)], axis=1)

    def dot(a, b):
        return jnp.dot(a, b, preferred_element_type=f32)

    def rotated(v, j, lo=0):
        n = v.shape[0]
        first_half = v[:, :128]
        swapped = jnp.where(
            lane[:n] < 32, pltpu.roll(first_half, 96, 1), pltpu.roll(first_half, 32, 1)
        )
        turned = first_half * ctab[j, lo : lo + n, :] + swapped * stab[j, lo : lo + n, :]
        return jnp.concatenate([turned, v[:, 128:]], axis=1)

    def each_head(body):
        pl.loop(0, HEADS)(body)

    def keys(j, lo=0, n=TOK):
        @each_head
        def _(h):
            kbuf[j % 2, h, lo : lo + n, :] = rotated(
                dot(H[j, lo : lo + n, :], columns(HEADS + h)), j, lo
            ).astype(bf16)

    def value_base(j):
        @each_head
        def _(h):
            vpre[j, h] = dot(H[j], columns(2 * HEADS + h))

    def query_base():
        @each_head
        def _(h):
            acc[h] = dot(H[0], columns(h))

    def ranks(j, lo=0, n=TOK):
        r = lax.dot_general(
            H[j, lo : lo + n, :], dsel[...], (((1,), (1,)), ((), ())), preferred_element_type=f32
        )
        column = lax.broadcasted_iota(i32, (n, 256), 1) // 16
        request = jnp.concatenate([owner[j, lo : lo + n, :]] * 2, axis=1)
        rbuf[lo : lo + n, :] = jnp.where(column == request, r, 0.0).astype(bf16)

    def delta(h, base, lo=0, n=TOK):
        u = usel[:, pl.ds(at(h * HS + base, HS), HS)]
        return adapter_scale_factor * dot(rbuf[lo : lo + n, :], u)

    def finish_query():
        @each_head
        def _(h):
            q = rotated(acc[h] + delta(h, 0), 0).astype(bf16)
            qbuf[h] = q * jnp.asarray(HS ** (-0.5), bf16)

    def values(j, lo=0, n=TOK):
        @each_head
        def _(h):
            if j < 2:
                base = vpre[j, h]
            else:
                base = dot(H[j, lo : lo + n, :], columns(2 * HEADS + h))
            vbuf[h, lo : lo + n, :] = (base + delta(h, WIDTH, lo, n)).astype(bf16)

    def attend(j, lo=0, n=TOK, last=False):
        begin = jnp.concatenate([begins[...]] * (n // 128), axis=1)
        row = lax.broadcasted_iota(i32, (TOK, n), 0) + s * TOK
        col = lax.broadcasted_iota(i32, (TOK, n), 1) + ((s - j) * TOK + lo)
        bias[:, :n] = jnp.where((col >= begin) & (col <= row), 0.0, -1e30).astype(f32)

        def piece(h, r):
            scores = lax.dot_general(
                qbuf[h, r, :], kbuf[j % 2, h, lo : lo + n, :], (((1,), (1,)), ((), ())),
                preferred_element_type=f32,
            ) + bias[r, :n]
            top = jnp.max(scores, axis=-1, keepdims=True)
            if j == 0:
                p = jnp.exp(scores - top)
                total = jnp.sum(p, axis=-1, keepdims=True)
                mixed = dot(p.astype(bf16), vbuf[h, lo : lo + n, :])
            else:
                before = mbuf[h, r, :][:, :1]
                top = jnp.maximum(top, before)
                fade = jnp.exp(before - top)
                p = jnp.exp(scores - top)
                total = fade * lbuf[h, r, :][:, :1] + jnp.sum(p, axis=-1, keepdims=True)
                mixed = fade * acc[h, r, :] + dot(p.astype(bf16), vbuf[h, lo : lo + n, :])
            if last:
                att[r, pl.ds(at(h * HS, HS), HS)] = (mixed / total).astype(bf16)
            else:
                acc[h, r, :] = mixed
                mbuf[h, r, :] = jnp.broadcast_to(top, (256, 128))
                lbuf[h, r, :] = jnp.broadcast_to(total, (256, 128))

        @pl.loop(0, HEADS // HEADS_AT_ONCE)
        def _(i):
            for o in range(HEADS_AT_ONCE):
                for k in range(2):
                    piece(i * HEADS_AT_ONCE + o, slice(k * 256, (k + 1) * 256))

    per_core(first)
    hop(1)
    per_core(first_rest)
    per_core(second)
    keys(0)
    query_base()
    per_core(third)
    @pl.when(z == 0)
    def _():
        hop(2)

    value_base(0)
    keys(1)
    per_core(fourth)
    value_base(1)

    @pl.when(z != 0)
    def _():
        hop(2)

    per_core(fifth)

    table = slots[...].astype(f32)
    at_slot = lax.broadcasted_iota(i32, (1, 64), 1)
    inner = lax.broadcasted_iota(i32, (16, 1024), 0)
    column = lax.broadcasted_iota(i32, (16, 1024), 1)
    for r in range(REQS):
        slot = jnp.sum(jnp.where(at_slot == ids[f, r], table, 0.0), axis=-1, keepdims=True)
        hit = column == slot.astype(i32) * 16 + inner
        onehot[r * 16 : (r + 1) * 16, :] = jnp.where(hit, 1.0, 0.0).astype(bf16)

    for g in range(8):
        for n, picked in ((1, dsel), (2, usel)):
            picked[:, g * 256 : (g + 1) * 256] = jnp.dot(
                onehot[...], ws[g % 2, g // 2, n], preferred_element_type=f32
            ).astype(bf16)

    ranks(0)
    finish_query()
    values(0)
    attend(0)
    ranks(1)
    values(1)
    attend(1)
    keys(2)
    ranks(2)
    values(2)
    attend(2)
    for k in range(2):
        arrived(part(3, k), ("halo", 2, k))
        keys(3, k * half, half)
        ranks(3, k * half, half)
        values(3, k * half, half)
        attend(3, k * half, half, last=k == 1)

    def store(g):
        return pltpu.make_async_copy(obuf.at[g % 2], out.at[:, pl.ds(g * 256, 256)], osem.at[g % 2])

    for g in range(8):
        if g >= 2:
            store(g - 2).wait()
        obuf[g % 2] = dot(att[...], ws[g % 2, g // 2, 0]).astype(bf16)
        store(g).start()
    for g in (6, 7):
        store(g).wait()

    for n in range(SPAN):
        for k in range(2):
            departed(part(n, k), ("halo", n, k))
    for k in range(NZ - 1):
        departed(piece_q(k), ("zq", k))
        departed(piece_s(k), ("zs", k))
    per_core(drain)


def run_whole(lengths, ids, slots, inverse, tokens, qkv_weight, out_weight, down, up):
    anywhere = pl.BlockSpec(memory_space=pl.ANY)
    scalar = pl.BlockSpec(memory_space=pltpu.SMEM)
    return pl.pallas_call(
        whole_kernel,
        out_shape=jax.ShapeDtypeStruct((TOK, 2 * WIDTH), bf16),
        in_specs=[scalar] * 2 + [pl.BlockSpec(memory_space=pltpu.VMEM)] * 2 + [anywhere] * 5,
        out_specs=anywhere,
        scratch_shapes=[
            pltpu.VMEM((2, NX, 3, 2048, 128), bf16),
            pltpu.VMEM((2, NX, 3, 1024, 256), bf16),
            pltpu.VMEM((SPAN + 1, TOK, 2048), bf16),
            pltpu.VMEM((2, HEADS, TOK, HS), bf16),
            pltpu.VMEM((HEADS, TOK, HS), bf16),
            pltpu.VMEM((HEADS, TOK, HS), bf16),
            pltpu.VMEM((256, 1024), bf16),
            pltpu.VMEM((256, 2048), bf16),
            pltpu.VMEM((256, 2048), bf16),
            pltpu.VMEM((TOK, 256), bf16),
            pltpu.VMEM((HEADS, TOK, HS), f32),
            pltpu.VMEM((2, HEADS, TOK, HS), f32),
            pltpu.VMEM((HEADS, TOK, 128), f32),
            pltpu.VMEM((HEADS, TOK, 128), f32),
            pltpu.VMEM((SPAN + 1, TOK, 128), f32),
            pltpu.VMEM((SPAN + 1, TOK, 128), f32),
            pltpu.VMEM((TOK, 128), i32),
            pltpu.VMEM((SPAN + 1, TOK, 128), i32),
            pltpu.VMEM((TOK, TOK), f32),
            pltpu.VMEM((2, TOK, 256), bf16),
            pltpu.VMEM((TOK, WIDTH), bf16),
            pltpu.SemaphoreType.DMA((130,)),
            pltpu.SemaphoreType.DMA((130,)),
            pltpu.SemaphoreType.DMA((8,)),
            pltpu.SemaphoreType.DMA((2,)),
        ],
        compiler_params=pltpu.CompilerParams(
            collective_id=0, has_side_effects=True, vmem_limit_bytes=63 * 1024 * 1024
        ),
    )(lengths, ids, slots, inverse, tokens, qkv_weight, out_weight, down, up)


def per_device(
    tokens, qkv_weight, out_weight, adapter_down, adapter_up, lengths, adapter_ids, adapter_slot
):
    rotary = HS // 4
    inverse = 10000.0 ** (-2.0 * (np.arange(128) % (rotary // 2)) / rotary)
    inverse = jnp.asarray(np.tile(inverse[None, :], (8, 1)), f32)
    return run_whole(
        lengths, adapter_ids, adapter_slot.reshape(1, -1), inverse, tokens, qkv_weight, out_weight,
        adapter_down.reshape(-1, 2048), adapter_up.reshape(-1, 2048),
    )


def solution(mesh):
    in_specs = (
        P(("fsdp", "seq"), None),
        P("seq", "fsdp"),
        P("seq", "fsdp"),
        P("seq", None, None),
        P("seq", None, None),
        P(),
        P(),
        P(),
    )
    out_specs = P(("fsdp", "seq"), None)
    return jax.shard_map(
        per_device, mesh=mesh, in_specs=in_specs, out_specs=out_specs, check_vma=False
    )
```

```python
import functools

import jax
import jax.numpy as jnp
import numpy as np
from jax import lax
from jax.experimental import pallas as pl
from jax.experimental.pallas import tpu as pltpu
from jax.sharding import PartitionSpec as P

HS = 256
HEADS = 4
SPAN = 3
TOK = 512
REQS = 16
WIDTH = 1024
NX, NY, NZ = 4, 4, 8
MESH = pl.DeviceIdType.MESH
HEADS_AT_ONCE = 2
OUT_AT_ONCE = 2
DETOUR = True
bf16, f32, i32 = jnp.bfloat16, jnp.float32, jnp.int32

eps_norm = 1e-05
adapter_scale_factor = 0.5


def whole_kernel(
    lengths, ids, slots, inverse, tokens, qkv, outw, down, up,
    out,
    wq, ws, H, kbuf, vbuf, qbuf, onehot, dsel, usel, rbuf, acc, vpre, mbuf, lbuf, ctab, stab, begins, owner, bias, obuf, att,
    send, recv, local, osem,
):
    f = lax.axis_index("fsdp")
    s = lax.axis_index("seq")
    x, c = f // 2, lax.rem(f, 2)
    y, z = s // NZ, lax.rem(s, NZ)
    xs = {d: lax.rem(x + d + NX, NX) for d in (-1, 0, 1, 2)}
    ys = {d: lax.rem(y + d + NY, NY) for d in (-1, 0, 1, 2)}
    zs = {d: lax.rem(z + d, NZ) for d in range(NZ)}
    at = pl.multiple_of
    dev_x = {d: {"fsdp": xs[d] * 2 + c, "seq": s} for d in (1, -1)}
    dev_y = {d: {"fsdp": f, "seq": ys[d] * NZ + z} for d in (1, -1)}
    dev_z = {d: {"fsdp": f, "seq": y * NZ + zs[d % NZ]} for d in (1, -1)}
    dev_c = {"fsdp": x * 2 + (1 - c), "seq": s}
    self_id = {"fsdp": f, "seq": s}

    q_piece = {d: at((y * NZ + zs[d]) * 64, 64) for d in range(NZ)}
    s_piece = {d: at((y * NZ + zs[d]) * 32, 32) for d in range(NZ)}
    q_rows = {d: {h: at(ys[d] * 512 + o, 256) for h, o in ((None, 0), (0, 0), (1, 256))} for d in ys}
    s_rows = {d: {h: at(ys[d] * 256 + o, 128) for h, o in ((None, 0), (0, 0), (1, 128))} for d in ys}
    cols = pl.ds(at(f * 256, 256), 256)

    load = pltpu.make_async_copy(tokens, H.at[0], local.at[4])
    load.start()

    def piece_q(d):
        return wq.at[c, x, :, pl.ds(q_piece[d], 64), :]

    def piece_s(d):
        return ws.at[c, x, :, pl.ds(s_piece[d], 32), :]

    parts = {1: pl.ds(1, 2), 2: pl.ds(0, 1)}

    own = [
        pltpu.make_async_copy(outw, piece_s(0).at[0], local.at[0]),
        pltpu.make_async_copy(down.at[:, cols], piece_s(0).at[1], local.at[1]),
        pltpu.make_async_copy(up.at[:, cols], piece_s(0).at[2], local.at[2]),
    ] + [
        pltpu.make_async_copy(qkv.at[:, pl.ds(t * 128, 128)], piece_q(0).at[t], local.at[5 + t])
        for t in range(3)
    ]
    for copy in own:
        copy.start()

    barrier = pltpu.get_barrier_semaphore()
    total = NY * NZ
    following = {"fsdp": f, "seq": lax.rem(s + 1, total)}
    preceding = {"fsdp": f, "seq": lax.rem(s + total - 1, total)}
    peers = [following, preceding, dev_x[1], dev_x[-1], dev_y[1], dev_y[-1], dev_z[1], dev_z[-1], dev_c]
    for peer in peers:
        pl.semaphore_signal(barrier, inc=1, device_id=peer, device_id_type=MESH)
    pl.semaphore_wait(barrier, len(peers))

    names = {}

    def sem_of(name):
        return names.setdefault(name, len(names))

    def push(src, dst, name, peer, recv_name=None):
        copy = pltpu.make_async_remote_copy(
            src_ref=src, dst_ref=dst,
            send_sem=send.at[sem_of(name)], recv_sem=recv.at[sem_of(recv_name or name)],
            device_id=peer, device_id_type=MESH,
        )
        copy.start()
        return copy

    def arrived(dst, name):
        i = sem_of(name)
        pltpu.make_async_remote_copy(
            src_ref=dst, dst_ref=dst, send_sem=send.at[i], recv_sem=recv.at[i],
            device_id=self_id, device_id_type=MESH,
        ).wait_recv()

    def departed(src, name):
        i = sem_of(name)
        pltpu.make_async_remote_copy(
            src_ref=src, dst_ref=src, send_sem=send.at[i], recv_sem=recv.at[i],
            device_id=self_id, device_id_type=MESH,
        ).wait_send()

    half = TOK // 2

    def part(n, k):
        return H.at[n, pl.ds(k * half, half), :]

    def hop_part(n, k):
        push(part(n, k), part(n + 1, k), ("halo", n, k), following)

    def hop(n):
        for k in range(2):
            arrived(part(n, k), ("halo", n - 1, k))
            hop_part(n, k)

    lane = lax.broadcasted_iota(i32, (TOK, 128), 1)
    token = lax.broadcasted_iota(i32, (TOK, 128), 0)

    def norm(k):
        @pl.loop(0, half // 64)
        def _(i):
            r = pl.ds(at(k * half + i * 64, 64), 64)
            v = H[0, r, :].astype(f32)
            mean = jnp.mean(v, axis=-1, keepdims=True)
            centred = v - mean
            variance = jnp.mean(centred * centred, axis=-1, keepdims=True)
            H[0, r, :] = (centred * lax.rsqrt(variance + eps_norm)).astype(bf16)

    def tables(j):
        position = (s - j) * TOK + token
        ends = jnp.int32(0)
        begin = jnp.zeros((TOK, 128), i32)
        request = jnp.zeros((TOK, 128), i32)
        for r in range(REQS - 1):
            ends = ends + lengths[f, r]
            past = position >= ends
            begin = jnp.where(past, ends, begin)
            request = request + past.astype(i32)
        if j == 0:
            begins[...] = begin
        owner[j] = request
        angle = (position - begin).astype(f32) * inverse[0:1, :]
        ctab[j] = jnp.where(lane < 64, jnp.cos(angle), 1.0)
        sine = jnp.sin(angle)
        stab[j] = jnp.where(lane < 32, -sine, jnp.where(lane < 64, sine, 0.0))

    def z_step(k):
        for name, piece in (("zq", piece_q), ("zs", piece_s)):
            if k > 0:
                arrived(piece(k), (name, k - 1))
            push(piece(k), piece(k), (name, k), dev_z[-1])

    load.wait()
    norm(0)
    hop_part(0, 0)
    for copy in own:
        copy.wait()
    z_step(0)
    norm(1)
    hop_part(0, 1)
    z_step(1)
    for k in range(2, NZ - 1):
        z_step(k)
        if k - 2 <= SPAN:
            tables(k - 2)

    def end_z(name, piece):
        arrived(piece(NZ - 1), (name, NZ - 2))

    def mid_y(d, h, a):
        if a == 0:
            return wq.at[c, x, :, pl.ds(q_rows[d][h], 256), :]
        return ws.at[c, x, parts[a], pl.ds(s_rows[d][h], 128), :]

    def mid_x(d, h, a):
        if a == 0:
            return wq.at[c, xs[d], :, pl.ds(q_rows[0][h], 256), :]
        return ws.at[c, xs[d], parts[a], pl.ds(s_rows[0][h], 128), :]

    def last_x(cc, d, h, a):
        if a == 0:
            return wq.at[cc, xs[d]] if h is None else wq.at[cc, xs[d], :, pl.ds(h * 1024, 1024), :]
        base, size = (0, 1024) if h is None else (h * 512, 512)
        return ws.at[cc, xs[d], parts[a], pl.ds(base, size), :]

    def last_y(cc, d, h, a):
        if a == 0:
            return wq.at[cc, :, :, pl.ds(q_rows[d][h], 512 if h is None else 256), :]
        return ws.at[cc, :, parts[a], pl.ds(s_rows[d][h], 256 if h is None else 128), :]

    inner_plane = z != 0

    class Ring:
        def __init__(self, pick, devs, tag, detour=False):
            self.pick, self.devs, self.tag, self.detour = pick, devs, tag, detour

        def send(self, d, h, a, name, k):
            if self.detour and k == 1:
                @pl.when(inner_plane)
                def _():
                    push(self.pick(d, h, a), self.pick(d, h, a), name, self.devs[k])
            else:
                push(self.pick(d, h, a), self.pick(d, h, a), name, self.devs[k])

        def get(self, d, h, a, name, k):
            arrived(self.pick(d, h, a), name)
            if self.detour and k == 1:
                @pl.when(z == 1)
                def _():
                    push(self.pick(d, h, a), self.pick(d, h, a), ("detour",) + name, dev_z[-1], name)

        def begin(self, a):
            for h, k in ((0, 1), (1, -1), (1, 1), (0, -1)):
                self.send(0, h, a, (self.tag, "own", k, h, a), k)

        def forward(self, a):
            for k, h in ((1, 0), (-1, 1)):
                self.get(-k, h, a, (self.tag, "own", k, h, a), k)
                self.send(-k, h, a, (self.tag, "fwd", k, a), k)

        def near(self, a):
            for k, h in ((1, 1), (-1, 0)):
                self.get(-k, h, a, (self.tag, "own", k, h, a), k)

        def far(self, a):
            for k, h in ((1, 0), (-1, 1)):
                self.get(2, h, a, (self.tag, "fwd", k, a), k)

        def left(self, d, h, a, name, k):
            if self.detour and k == 1:
                @pl.when(inner_plane)
                def _():
                    departed(self.pick(d, h, a), name)
            else:
                departed(self.pick(d, h, a), name)

        def drain(self):
            for a in range(3):
                for h, k in ((0, 1), (1, -1), (1, 1), (0, -1)):
                    self.left(0, h, a, (self.tag, "own", k, h, a), k)
                for k, h in ((1, 0), (-1, 1)):
                    self.left(-k, h, a, (self.tag, "fwd", k, a), k)
                if self.detour:
                    @pl.when(z == 1)
                    def _():
                        for d, h, name in (
                            (-1, 0, (self.tag, "own", 1, 0, a)),
                            (-1, 1, (self.tag, "own", 1, 1, a)),
                            (2, 0, (self.tag, "fwd", 1, a)),
                        ):
                            departed(self.pick(d, h, a), ("detour",) + name)

    plans = []
    for cc, mid, mid_devs, last, last_devs, other in (
        (0, mid_y, dev_y, last_x, dev_x, last_y),
        (1, mid_x, dev_x, last_y, dev_y, last_x),
    ):
        plans.append((
            Ring(mid, mid_devs, "mid", detour=DETOUR and cc == 0),
            Ring(functools.partial(last, cc), last_devs, "last", detour=DETOUR and cc == 1),
            functools.partial(last, cc),
            functools.partial(other, 1 - cc),
            cc,
        ))

    def per_core(body):
        for plan in plans:
            @pl.when(c == plan[4])
            def _():
                body(*plan)

    def share(give, cc, a, *ds):
        for d in ds:
            push(give(d, None, a), give(d, None, a), ("core", d, a, cc), dev_c)

    def first(mid, last, give, take, cc):
        end_z("zq", piece_q)
        mid.begin(0)
        end_z("zs", piece_s)
        mid.forward(0)
        mid.begin(1)
        mid.near(0)
        mid.far(0)
        last.begin(0)
        share(give, cc, 0, 0)

    def first_rest(mid, last, give, take, cc):
        mid.forward(1)
        mid.begin(2)
        mid.near(1)
        mid.far(1)
        last.forward(0)
        last.begin(1)
        share(give, cc, 1, 0)
        mid.forward(2)

    def second(mid, last, give, take, cc):
        last.near(0)
        share(give, cc, 0, -1, 1)
        mid.near(2)
        mid.far(2)
        last.far(0)
        share(give, cc, 0, 2)
        receive(take, cc, 0)

    def receive(take, cc, a):
        for d in (0, -1, 1, 2):
            arrived(take(d, None, a), ("core", d, a, 1 - cc))

    def third(mid, last, give, take, cc):
        last.forward(1)
        last.begin(2)
        share(give, cc, 2, 0)

    def fourth(mid, last, give, take, cc):
        last.near(1)
        share(give, cc, 1, -1, 1)

    def fifth(mid, last, give, take, cc):
        last.far(1)
        share(give, cc, 1, 2)
        receive(take, cc, 1)

    def out_second(mid, last, give, take, cc):
        last.forward(2)

    def out_third(mid, last, give, take, cc):
        last.near(2)
        share(give, cc, 2, -1, 1)

    def out_last(mid, last, give, take, cc):
        last.far(2)
        share(give, cc, 2, 2)

    def out_received(mid, last, give, take, cc):
        receive(take, cc, 2)

    def drain(mid, last, give, take, cc):
        mid.drain()
        last.drain()
        for a in range(3):
            for d in (0, -1, 1, 2):
                departed(give(d, None, a), ("core", d, a, cc))

    def weight(tile):
        g = tile // 3
        return wq[lax.rem(g, 2), g // 2, lax.rem(tile, 3)]

    def columns(head):
        return jnp.concatenate([weight(2 * head), weight(2 * head + 1)], axis=1)

    def dot(a, b):
        return jnp.dot(a, b, preferred_element_type=f32)

    def rotated(v, j, lo=0):
        n = v.shape[0]
        first_half = v[:, :128]
        swapped = jnp.where(
            lane[:n] < 32, pltpu.roll(first_half, 96, 1), pltpu.roll(first_half, 32, 1)
        )
        turned = first_half * ctab[j, lo : lo + n, :] + swapped * stab[j, lo : lo + n, :]
        return jnp.concatenate([turned, v[:, 128:]], axis=1)

    def each_head(body):
        pl.loop(0, HEADS)(body)

    def keys(j, lo=0, n=TOK):
        @each_head
        def _(h):
            kbuf[j % 2, h, lo : lo + n, :] = rotated(
                dot(H[j, lo : lo + n, :], columns(HEADS + h)), j, lo
            ).astype(bf16)

    def value_base(j):
        @each_head
        def _(h):
            vpre[j, h] = dot(H[j], columns(2 * HEADS + h))

    def query_base():
        @each_head
        def _(h):
            acc[h] = dot(H[0], columns(h))

    def ranks(j, lo=0, n=TOK):
        r = lax.dot_general(
            H[j, lo : lo + n, :], dsel[...], (((1,), (1,)), ((), ())), preferred_element_type=f32
        )
        column = lax.broadcasted_iota(i32, (n, 256), 1) // 16
        request = jnp.concatenate([owner[j, lo : lo + n, :]] * 2, axis=1)
        rbuf[lo : lo + n, :] = jnp.where(column == request, r, 0.0).astype(bf16)

    def delta(h, base, lo=0, n=TOK):
        u = usel[:, pl.ds(at(h * HS + base, HS), HS)]
        return adapter_scale_factor * dot(rbuf[lo : lo + n, :], u)

    def finish_query():
        @each_head
        def _(h):
            q = rotated(acc[h] + delta(h, 0), 0).astype(bf16)
            qbuf[h] = q * jnp.asarray(HS ** (-0.5), bf16)

    def values(j, lo=0, n=TOK):
        @each_head
        def _(h):
            if j < 2:
                base = vpre[j, h]
            else:
                base = dot(H[j, lo : lo + n, :], columns(2 * HEADS + h))
            vbuf[h, lo : lo + n, :] = (base + delta(h, WIDTH, lo, n)).astype(bf16)

    def set_bias(j, lo, n):
        begin = jnp.concatenate([begins[...]] * (n // 128), axis=1)
        row = lax.broadcasted_iota(i32, (TOK, n), 0) + s * TOK
        col = lax.broadcasted_iota(i32, (TOK, n), 1) + ((s - j) * TOK + lo)
        bias[:, :n] = jnp.where((col >= begin) & (col <= row), 0.0, -1e30).astype(f32)

    def soften(h, r, key, value, first=False, last=False):
        scores = lax.dot_general(
            qbuf[h, r, :], key, (((1,), (1,)), ((), ())), preferred_element_type=f32
        ) + bias[r, : key.shape[0]]
        top = jnp.max(scores, axis=-1, keepdims=True)
        if first:
            p = jnp.exp(scores - top)
            total = jnp.sum(p, axis=-1, keepdims=True)
            mixed = dot(p.astype(bf16), value)
        else:
            before = mbuf[h, r, :][:, :1]
            top = jnp.maximum(top, before)
            fade = jnp.exp(before - top)
            p = jnp.exp(scores - top)
            total = fade * lbuf[h, r, :][:, :1] + jnp.sum(p, axis=-1, keepdims=True)
            mixed = fade * acc[h, r, :] + dot(p.astype(bf16), value)
        if last:
            att[r, pl.ds(at(h * HS, HS), HS)] = (mixed / total).astype(bf16)
        else:
            acc[h, r, :] = mixed
            mbuf[h, r, :] = jnp.broadcast_to(top, (256, 128))
            lbuf[h, r, :] = jnp.broadcast_to(total, (256, 128))

    tiles = (slice(0, 256), slice(256, 512))

    def attend(j):
        set_bias(j, 0, TOK)

        @each_head
        def _(h):
            for r in tiles:
                soften(h, r, kbuf[j % 2, h], vbuf[h], first=j == 0)

    def project_and_attend(j, lo, n, last):
        set_bias(j, lo, n)
        ranks(j, lo, n)

        @pl.loop(0, HEADS // HEADS_AT_ONCE)
        def _(i):
            for o in range(HEADS_AT_ONCE):
                h = i * HEADS_AT_ONCE + o
                rows = H[j, lo : lo + n, :]
                key = rotated(dot(rows, columns(HEADS + h)), j, lo).astype(bf16)
                value = (dot(rows, columns(2 * HEADS + h)) + delta(h, WIDTH, lo, n)).astype(bf16)
                for r in tiles:
                    soften(h, r, key, value, last=last)

    per_core(first)
    hop(1)
    per_core(first_rest)
    per_core(second)
    keys(0)
    query_base()
    per_core(third)
    @pl.when(z == 0)
    def _():
        hop(2)

    value_base(0)
    keys(1)
    per_core(fourth)
    value_base(1)

    @pl.when(z != 0)
    def _():
        hop(2)

    per_core(fifth)
    per_core(out_second)

    table = slots[...].astype(f32)
    at_slot = lax.broadcasted_iota(i32, (1, 64), 1)
    inner = lax.broadcasted_iota(i32, (16, 1024), 0)
    column = lax.broadcasted_iota(i32, (16, 1024), 1)
    for r in range(REQS):
        slot = jnp.sum(jnp.where(at_slot == ids[f, r], table, 0.0), axis=-1, keepdims=True)
        hit = column == slot.astype(i32) * 16 + inner
        onehot[r * 16 : (r + 1) * 16, :] = jnp.where(hit, 1.0, 0.0).astype(bf16)

    for g in range(8):
        for n, picked in ((1, dsel), (2, usel)):
            picked[:, g * 256 : (g + 1) * 256] = jnp.dot(
                onehot[...], ws[g % 2, g // 2, n], preferred_element_type=f32
            ).astype(bf16)

    ranks(0)
    finish_query()
    values(0)
    attend(0)
    per_core(out_third)
    ranks(1)
    values(1)
    attend(1)
    per_core(out_last)
    keys(2)
    ranks(2)
    values(2)
    attend(2)
    per_core(out_received)
    for k in range(2):
        arrived(part(3, k), ("halo", 2, k))
        project_and_attend(3, k * half, half, last=k == 1)

    def store(g):
        part_of = pl.ds(at(g * 256, 256), 256)
        return pltpu.make_async_copy(obuf.at[:, part_of], out.at[:, part_of], osem.at[g])

    @pl.loop(0, 8 // OUT_AT_ONCE)
    def _(i):
        for o in range(OUT_AT_ONCE):
            g = i * OUT_AT_ONCE + o
            obuf[:, pl.ds(at(g * 256, 256), 256)] = dot(
                att[...], ws[lax.rem(g, 2), g // 2, 0]
            ).astype(bf16)
            store(g).start()

    for g in range(8):
        store(g).wait()

    for n in range(SPAN):
        for k in range(2):
            departed(part(n, k), ("halo", n, k))
    for k in range(NZ - 1):
        departed(piece_q(k), ("zq", k))
        departed(piece_s(k), ("zs", k))
    per_core(drain)


def run_whole(lengths, ids, slots, inverse, tokens, qkv_weight, out_weight, down, up):
    anywhere = pl.BlockSpec(memory_space=pl.ANY)
    scalar = pl.BlockSpec(memory_space=pltpu.SMEM)
    return pl.pallas_call(
        whole_kernel,
        out_shape=jax.ShapeDtypeStruct((TOK, 2 * WIDTH), bf16),
        in_specs=[scalar] * 2 + [pl.BlockSpec(memory_space=pltpu.VMEM)] * 2 + [anywhere] * 5,
        out_specs=anywhere,
        scratch_shapes=[
            pltpu.VMEM((2, NX, 3, 2048, 128), bf16),
            pltpu.VMEM((2, NX, 3, 1024, 256), bf16),
            pltpu.VMEM((SPAN + 1, TOK, 2048), bf16),
            pltpu.VMEM((2, HEADS, TOK, HS), bf16),
            pltpu.VMEM((HEADS, TOK, HS), bf16),
            pltpu.VMEM((HEADS, TOK, HS), bf16),
            pltpu.VMEM((256, 1024), bf16),
            pltpu.VMEM((256, 2048), bf16),
            pltpu.VMEM((256, 2048), bf16),
            pltpu.VMEM((TOK, 256), bf16),
            pltpu.VMEM((HEADS, TOK, HS), f32),
            pltpu.VMEM((2, HEADS, TOK, HS), f32),
            pltpu.VMEM((HEADS, TOK, 128), f32),
            pltpu.VMEM((HEADS, TOK, 128), f32),
            pltpu.VMEM((SPAN + 1, TOK, 128), f32),
            pltpu.VMEM((SPAN + 1, TOK, 128), f32),
            pltpu.VMEM((TOK, 128), i32),
            pltpu.VMEM((SPAN + 1, TOK, 128), i32),
            pltpu.VMEM((TOK, TOK), f32),
            pltpu.VMEM((TOK, 2 * WIDTH), bf16),
            pltpu.VMEM((TOK, WIDTH), bf16),
            pltpu.SemaphoreType.DMA((190,)),
            pltpu.SemaphoreType.DMA((190,)),
            pltpu.SemaphoreType.DMA((8,)),
            pltpu.SemaphoreType.DMA((8,)),
        ],
        compiler_params=pltpu.CompilerParams(
            collective_id=0, has_side_effects=True, vmem_limit_bytes=63 * 1024 * 1024
        ),
    )(lengths, ids, slots, inverse, tokens, qkv_weight, out_weight, down, up)


def per_device(
    tokens, qkv_weight, out_weight, adapter_down, adapter_up, lengths, adapter_ids, adapter_slot
):
    rotary = HS // 4
    inverse = 10000.0 ** (-2.0 * (np.arange(128) % (rotary // 2)) / rotary)
    inverse = jnp.asarray(np.tile(inverse[None, :], (8, 1)), f32)
    return run_whole(
        lengths, adapter_ids, adapter_slot.reshape(1, -1), inverse, tokens, qkv_weight, out_weight,
        adapter_down.reshape(-1, 2048), adapter_up.reshape(-1, 2048),
    )


def solution(mesh):
    in_specs = (
        P(("fsdp", "seq"), None),
        P("seq", "fsdp"),
        P("seq", "fsdp"),
        P("seq", None, None),
        P("seq", None, None),
        P(),
        P(),
        P(),
    )
    out_specs = P(("fsdp", "seq"), None)
    return jax.shard_map(
        per_device, mesh=mesh, in_specs=in_specs, out_specs=out_specs, check_vma=False
    )
```

```python
import functools

import jax
import jax.numpy as jnp
import numpy as np
from jax import lax
from jax.experimental import pallas as pl
from jax.experimental.pallas import tpu as pltpu
from jax.sharding import PartitionSpec as P

HS = 256
HEADS = 4
SPAN = 3
TOK = 512
REQS = 16
WIDTH = 1024
NX, NY, NZ = 4, 4, 8
MESH = pl.DeviceIdType.MESH
HEADS_AT_ONCE = 2
PARTS = 2
OUT_AT_ONCE = 2
DETOUR = True
bf16, f32, i32 = jnp.bfloat16, jnp.float32, jnp.int32

eps_norm = 1e-05
adapter_scale_factor = 0.5


def whole_kernel(
    lengths, ids, slots, inverse, tokens, qkv, outw, down, up,
    out,
    wq, ws, H, kbuf, vbuf, qbuf, onehot, dsel, usel, rbuf, acc, vpre, mbuf, lbuf, ctab, stab, begins, owner, bias, obuf, att,
    send, recv, local, osem,
):
    f = lax.axis_index("fsdp")
    s = lax.axis_index("seq")
    x, c = f // 2, lax.rem(f, 2)
    y, z = s // NZ, lax.rem(s, NZ)
    xs = {d: lax.rem(x + d + NX, NX) for d in (-1, 0, 1, 2)}
    ys = {d: lax.rem(y + d + NY, NY) for d in (-1, 0, 1, 2)}
    zs = {d: lax.rem(z + d, NZ) for d in range(NZ)}
    at = pl.multiple_of
    dev_x = {d: {"fsdp": xs[d] * 2 + c, "seq": s} for d in (1, -1)}
    dev_y = {d: {"fsdp": f, "seq": ys[d] * NZ + z} for d in (1, -1)}
    dev_z = {d: {"fsdp": f, "seq": y * NZ + zs[d % NZ]} for d in (1, -1)}
    dev_c = {"fsdp": x * 2 + (1 - c), "seq": s}
    self_id = {"fsdp": f, "seq": s}

    q_piece = {d: at((y * NZ + zs[d]) * 64, 64) for d in range(NZ)}
    s_piece = {d: at((y * NZ + zs[d]) * 32, 32) for d in range(NZ)}
    q_rows = {d: {h: at(ys[d] * 512 + o, 256) for h, o in ((None, 0), (0, 0), (1, 256))} for d in ys}
    s_rows = {d: {h: at(ys[d] * 256 + o, 128) for h, o in ((None, 0), (0, 0), (1, 128))} for d in ys}
    cols = pl.ds(at(f * 256, 256), 256)

    load = pltpu.make_async_copy(tokens, H.at[0], local.at[4])
    load.start()

    def piece_q(d):
        return wq.at[c, x, :, pl.ds(q_piece[d], 64), :]

    def piece_s(d):
        return ws.at[c, x, :, pl.ds(s_piece[d], 32), :]

    parts = {1: pl.ds(1, 2), 2: pl.ds(0, 1)}

    own = [
        pltpu.make_async_copy(outw, piece_s(0).at[0], local.at[0]),
        pltpu.make_async_copy(down.at[:, cols], piece_s(0).at[1], local.at[1]),
        pltpu.make_async_copy(up.at[:, cols], piece_s(0).at[2], local.at[2]),
    ] + [
        pltpu.make_async_copy(qkv.at[:, pl.ds(t * 128, 128)], piece_q(0).at[t], local.at[5 + t])
        for t in range(3)
    ]
    for copy in own:
        copy.start()

    barrier = pltpu.get_barrier_semaphore()
    total = NY * NZ
    following = {"fsdp": f, "seq": lax.rem(s + 1, total)}
    preceding = {"fsdp": f, "seq": lax.rem(s + total - 1, total)}
    peers = [following, preceding, dev_x[1], dev_x[-1], dev_y[1], dev_y[-1], dev_z[1], dev_z[-1], dev_c]
    for peer in peers:
        pl.semaphore_signal(barrier, inc=1, device_id=peer, device_id_type=MESH)
    pl.semaphore_wait(barrier, len(peers))

    names = {}

    def sem_of(name):
        return names.setdefault(name, len(names))

    def push(src, dst, name, peer, recv_name=None):
        copy = pltpu.make_async_remote_copy(
            src_ref=src, dst_ref=dst,
            send_sem=send.at[sem_of(name)], recv_sem=recv.at[sem_of(recv_name or name)],
            device_id=peer, device_id_type=MESH,
        )
        copy.start()
        return copy

    def arrived(dst, name):
        i = sem_of(name)
        pltpu.make_async_remote_copy(
            src_ref=dst, dst_ref=dst, send_sem=send.at[i], recv_sem=recv.at[i],
            device_id=self_id, device_id_type=MESH,
        ).wait_recv()

    def departed(src, name):
        i = sem_of(name)
        pltpu.make_async_remote_copy(
            src_ref=src, dst_ref=src, send_sem=send.at[i], recv_sem=recv.at[i],
            device_id=self_id, device_id_type=MESH,
        ).wait_send()

    size = TOK // PARTS

    def part(n, k):
        return H.at[n, pl.ds(k * size, size), :]

    def hop_part(n, k):
        push(part(n, k), part(n + 1, k), ("halo", n, k), following)

    def hop(n, k):
        arrived(part(n, k), ("halo", n - 1, k))
        hop_part(n, k)

    lane = lax.broadcasted_iota(i32, (TOK, 128), 1)
    token = lax.broadcasted_iota(i32, (TOK, 128), 0)

    def norm(k):
        @pl.loop(0, size // 64)
        def _(i):
            r = pl.ds(at(k * size + i * 64, 64), 64)
            v = H[0, r, :].astype(f32)
            mean = jnp.mean(v, axis=-1, keepdims=True)
            centred = v - mean
            variance = jnp.mean(centred * centred, axis=-1, keepdims=True)
            H[0, r, :] = (centred * lax.rsqrt(variance + eps_norm)).astype(bf16)

    def tables(j):
        position = (s - j) * TOK + token
        ends = jnp.int32(0)
        begin = jnp.zeros((TOK, 128), i32)
        request = jnp.zeros((TOK, 128), i32)
        for r in range(REQS - 1):
            ends = ends + lengths[f, r]
            past = position >= ends
            begin = jnp.where(past, ends, begin)
            request = request + past.astype(i32)
        if j == 0:
            begins[...] = begin
        owner[j] = request
        angle = (position - begin).astype(f32) * inverse[0:1, :]
        ctab[j] = jnp.where(lane < 64, jnp.cos(angle), 1.0)
        sine = jnp.sin(angle)
        stab[j] = jnp.where(lane < 32, -sine, jnp.where(lane < 64, sine, 0.0))

    def z_step(k):
        for name, piece in (("zq", piece_q), ("zs", piece_s)):
            if k > 0:
                arrived(piece(k), (name, k - 1))
            push(piece(k), piece(k), (name, k), dev_z[-1])

    load.wait()
    norm(0)
    hop_part(0, 0)
    for copy in own:
        copy.wait()
    z_step(0)
    for k in range(1, PARTS):
        norm(k)
        hop_part(0, k)
    for k in range(1, NZ - 1):
        z_step(k)
        if 0 <= k - 2 <= SPAN:
            tables(k - 2)

    def end_z(name, piece):
        arrived(piece(NZ - 1), (name, NZ - 2))

    def mid_y(d, h, a):
        if a == 0:
            return wq.at[c, x, :, pl.ds(q_rows[d][h], 256), :]
        return ws.at[c, x, parts[a], pl.ds(s_rows[d][h], 128), :]

    def mid_x(d, h, a):
        if a == 0:
            return wq.at[c, xs[d], :, pl.ds(q_rows[0][h], 256), :]
        return ws.at[c, xs[d], parts[a], pl.ds(s_rows[0][h], 128), :]

    def last_x(cc, d, h, a):
        if a == 0:
            return wq.at[cc, xs[d]] if h is None else wq.at[cc, xs[d], :, pl.ds(h * 1024, 1024), :]
        base, size = (0, 1024) if h is None else (h * 512, 512)
        return ws.at[cc, xs[d], parts[a], pl.ds(base, size), :]

    def last_y(cc, d, h, a):
        if a == 0:
            return wq.at[cc, :, :, pl.ds(q_rows[d][h], 512 if h is None else 256), :]
        return ws.at[cc, :, parts[a], pl.ds(s_rows[d][h], 256 if h is None else 128), :]

    inner_plane = z != 0

    class Ring:
        def __init__(self, pick, devs, tag, detour=False):
            self.pick, self.devs, self.tag, self.detour = pick, devs, tag, detour

        def send(self, d, h, a, name, k):
            if self.detour and k == 1:
                @pl.when(inner_plane)
                def _():
                    push(self.pick(d, h, a), self.pick(d, h, a), name, self.devs[k])
            else:
                push(self.pick(d, h, a), self.pick(d, h, a), name, self.devs[k])

        def get(self, d, h, a, name, k):
            arrived(self.pick(d, h, a), name)
            if self.detour and k == 1:
                @pl.when(z == 1)
                def _():
                    push(self.pick(d, h, a), self.pick(d, h, a), ("detour",) + name, dev_z[-1], name)

        def begin(self, a):
            for h, k in ((0, 1), (1, -1), (1, 1), (0, -1)):
                self.send(0, h, a, (self.tag, "own", k, h, a), k)

        def forward(self, a):
            for k, h in ((1, 0), (-1, 1)):
                self.get(-k, h, a, (self.tag, "own", k, h, a), k)
                self.send(-k, h, a, (self.tag, "fwd", k, a), k)

        def near(self, a):
            for k, h in ((1, 1), (-1, 0)):
                self.get(-k, h, a, (self.tag, "own", k, h, a), k)

        def far(self, a):
            for k, h in ((1, 0), (-1, 1)):
                self.get(2, h, a, (self.tag, "fwd", k, a), k)

        def left(self, d, h, a, name, k):
            if self.detour and k == 1:
                @pl.when(inner_plane)
                def _():
                    departed(self.pick(d, h, a), name)
            else:
                departed(self.pick(d, h, a), name)

        def drain(self):
            for a in range(3):
                for h, k in ((0, 1), (1, -1), (1, 1), (0, -1)):
                    self.left(0, h, a, (self.tag, "own", k, h, a), k)
                for k, h in ((1, 0), (-1, 1)):
                    self.left(-k, h, a, (self.tag, "fwd", k, a), k)
                if self.detour:
                    @pl.when(z == 1)
                    def _():
                        for d, h, name in (
                            (-1, 0, (self.tag, "own", 1, 0, a)),
                            (-1, 1, (self.tag, "own", 1, 1, a)),
                            (2, 0, (self.tag, "fwd", 1, a)),
                        ):
                            departed(self.pick(d, h, a), ("detour",) + name)

    plans = []
    for cc, mid, mid_devs, last, last_devs, other in (
        (0, mid_y, dev_y, last_x, dev_x, last_y),
        (1, mid_x, dev_x, last_y, dev_y, last_x),
    ):
        plans.append((
            Ring(mid, mid_devs, "mid", detour=DETOUR and cc == 0),
            Ring(functools.partial(last, cc), last_devs, "last", detour=DETOUR and cc == 1),
            functools.partial(last, cc),
            functools.partial(other, 1 - cc),
            cc,
        ))

    def per_core(body):
        for plan in plans:
            @pl.when(c == plan[4])
            def _():
                body(*plan)

    def share(give, cc, a, *ds):
        for d in ds:
            push(give(d, None, a), give(d, None, a), ("core", d, a, cc), dev_c)

    def first(mid, last, give, take, cc):
        end_z("zq", piece_q)
        mid.begin(0)
        end_z("zs", piece_s)
        mid.forward(0)
        mid.begin(1)
        mid.near(0)
        mid.far(0)
        last.begin(0)
        share(give, cc, 0, 0)

    def first_rest(mid, last, give, take, cc):
        mid.forward(1)
        mid.begin(2)
        mid.near(1)
        mid.far(1)
        last.forward(0)
        last.begin(1)
        share(give, cc, 1, 0)
        mid.forward(2)

    def second(mid, last, give, take, cc):
        last.near(0)
        share(give, cc, 0, -1, 1)
        mid.near(2)
        mid.far(2)
        last.far(0)
        share(give, cc, 0, 2)
        receive(take, cc, 0)

    def receive(take, cc, a):
        for d in (0, -1, 1, 2):
            arrived(take(d, None, a), ("core", d, a, 1 - cc))

    def third(mid, last, give, take, cc):
        last.forward(1)
        last.begin(2)
        share(give, cc, 2, 0)

    def fourth(mid, last, give, take, cc):
        last.near(1)
        share(give, cc, 1, -1, 1)

    def fifth(mid, last, give, take, cc):
        last.far(1)
        share(give, cc, 1, 2)
        receive(take, cc, 1)

    def out_second(mid, last, give, take, cc):
        last.forward(2)

    def out_third(mid, last, give, take, cc):
        last.near(2)
        share(give, cc, 2, -1, 1)

    def out_last(mid, last, give, take, cc):
        last.far(2)
        share(give, cc, 2, 2)

    def out_received(mid, last, give, take, cc):
        receive(take, cc, 2)

    def drain(mid, last, give, take, cc):
        mid.drain()
        last.drain()
        for a in range(3):
            for d in (0, -1, 1, 2):
                departed(give(d, None, a), ("core", d, a, cc))

    def weight(tile):
        g = tile // 3
        return wq[lax.rem(g, 2), g // 2, lax.rem(tile, 3)]

    def columns(head):
        return jnp.concatenate([weight(2 * head), weight(2 * head + 1)], axis=1)

    def dot(a, b):
        return jnp.dot(a, b, preferred_element_type=f32)

    def rotated(v, j, lo=0):
        n = v.shape[0]
        first_half = v[:, :128]
        swapped = jnp.where(
            lane[:n] < 32, pltpu.roll(first_half, 96, 1), pltpu.roll(first_half, 32, 1)
        )
        turned = first_half * ctab[j, lo : lo + n, :] + swapped * stab[j, lo : lo + n, :]
        return jnp.concatenate([turned, v[:, 128:]], axis=1)

    def each_head(body):
        pl.loop(0, HEADS)(body)

    def keys(j, lo=0, n=TOK):
        @each_head
        def _(h):
            kbuf[j % 2, h, lo : lo + n, :] = rotated(
                dot(H[j, lo : lo + n, :], columns(HEADS + h)), j, lo
            ).astype(bf16)

    def value_base(j):
        @each_head
        def _(h):
            vpre[j, h] = dot(H[j], columns(2 * HEADS + h))

    def query_base():
        @each_head
        def _(h):
            acc[h] = dot(H[0], columns(h))

    def ranks(j, lo=0, n=TOK):
        r = lax.dot_general(
            H[j, lo : lo + n, :], dsel[...], (((1,), (1,)), ((), ())), preferred_element_type=f32
        )
        column = lax.broadcasted_iota(i32, (n, 256), 1) // 16
        request = jnp.concatenate([owner[j, lo : lo + n, :]] * 2, axis=1)
        rbuf[lo : lo + n, :] = jnp.where(column == request, r, 0.0).astype(bf16)

    def delta(h, base, lo=0, n=TOK):
        u = usel[:, pl.ds(at(h * HS + base, HS), HS)]
        return adapter_scale_factor * dot(rbuf[lo : lo + n, :], u)

    def finish_query():
        @each_head
        def _(h):
            q = rotated(acc[h] + delta(h, 0), 0).astype(bf16)
            qbuf[h] = q * jnp.asarray(HS ** (-0.5), bf16)

    def values(j, lo=0, n=TOK):
        @each_head
        def _(h):
            if j < 2:
                base = vpre[j, h]
            else:
                base = dot(H[j, lo : lo + n, :], columns(2 * HEADS + h))
            vbuf[h, lo : lo + n, :] = (base + delta(h, WIDTH, lo, n)).astype(bf16)

    def set_bias(j, lo, n):
        begin = jnp.concatenate([begins[...]] * (n // 128), axis=1)
        row = lax.broadcasted_iota(i32, (TOK, n), 0) + s * TOK
        col = lax.broadcasted_iota(i32, (TOK, n), 1) + ((s - j) * TOK + lo)
        bias[:, :n] = jnp.where((col >= begin) & (col <= row), 0.0, -1e30).astype(f32)

    def soften(h, r, key, value, first=False, last=False):
        scores = lax.dot_general(
            qbuf[h, r, :], key, (((1,), (1,)), ((), ())), preferred_element_type=f32
        ) + bias[r, : key.shape[0]]
        top = jnp.max(scores, axis=-1, keepdims=True)
        if first:
            p = jnp.exp(scores - top)
            total = jnp.sum(p, axis=-1, keepdims=True)
            mixed = dot(p.astype(bf16), value)
        else:
            before = mbuf[h, r, :][:, :1]
            top = jnp.maximum(top, before)
            fade = jnp.exp(before - top)
            p = jnp.exp(scores - top)
            total = fade * lbuf[h, r, :][:, :1] + jnp.sum(p, axis=-1, keepdims=True)
            mixed = fade * acc[h, r, :] + dot(p.astype(bf16), value)
        if last:
            att[r, pl.ds(at(h * HS, HS), HS)] = (mixed / total).astype(bf16)
        else:
            acc[h, r, :] = mixed
            mbuf[h, r, :] = jnp.broadcast_to(top, (256, 128))
            lbuf[h, r, :] = jnp.broadcast_to(total, (256, 128))

    tiles = (slice(0, 256), slice(256, 512))

    def attend(j):
        set_bias(j, 0, TOK)

        @each_head
        def _(h):
            for r in tiles:
                soften(h, r, kbuf[j % 2, h], vbuf[h], first=j == 0)

    def project_and_attend(j, lo, n, last):
        set_bias(j, lo, n)
        ranks(j, lo, n)

        @pl.loop(0, HEADS // HEADS_AT_ONCE)
        def _(i):
            for o in range(HEADS_AT_ONCE):
                h = i * HEADS_AT_ONCE + o
                rows = H[j, lo : lo + n, :]
                key = rotated(dot(rows, columns(HEADS + h)), j, lo).astype(bf16)
                value = (dot(rows, columns(2 * HEADS + h)) + delta(h, WIDTH, lo, n)).astype(bf16)
                for r in tiles:
                    soften(h, r, key, value, last=last)

    per_core(first)
    hop(1, 0)
    per_core(first_rest)
    hop(1, 1)
    per_core(second)
    keys(0)
    query_base()
    per_core(third)
    hop(2, 0)
    value_base(0)
    keys(1)
    per_core(fourth)
    value_base(1)
    hop(2, 1)
    per_core(fifth)
    per_core(out_second)

    table = slots[...].astype(f32)
    at_slot = lax.broadcasted_iota(i32, (1, 64), 1)
    inner = lax.broadcasted_iota(i32, (16, 1024), 0)
    column = lax.broadcasted_iota(i32, (16, 1024), 1)
    for r in range(REQS):
        slot = jnp.sum(jnp.where(at_slot == ids[f, r], table, 0.0), axis=-1, keepdims=True)
        hit = column == slot.astype(i32) * 16 + inner
        onehot[r * 16 : (r + 1) * 16, :] = jnp.where(hit, 1.0, 0.0).astype(bf16)

    for g in range(8):
        for n, picked in ((1, dsel), (2, usel)):
            picked[:, g * 256 : (g + 1) * 256] = jnp.dot(
                onehot[...], ws[g % 2, g // 2, n], preferred_element_type=f32
            ).astype(bf16)

    ranks(0)
    finish_query()
    values(0)
    attend(0)
    per_core(out_third)
    ranks(1)
    values(1)
    attend(1)
    per_core(out_last)
    keys(2)
    ranks(2)
    values(2)
    attend(2)
    per_core(out_received)
    for ks in ((0,), (1,)):
        for k in ks:
            arrived(part(3, k), ("halo", 2, k))
        project_and_attend(3, ks[0] * size, len(ks) * size, last=ks[-1] == PARTS - 1)

    def store(g):
        part_of = pl.ds(at(g * 256, 256), 256)
        return pltpu.make_async_copy(obuf.at[:, part_of], out.at[:, part_of], osem.at[g])

    @pl.loop(0, 8 // OUT_AT_ONCE)
    def _(i):
        for o in range(OUT_AT_ONCE):
            g = i * OUT_AT_ONCE + o
            obuf[:, pl.ds(at(g * 256, 256), 256)] = dot(
                att[...], ws[lax.rem(g, 2), g // 2, 0]
            ).astype(bf16)
            store(g).start()

    for g in range(8):
        store(g).wait()

    for n in range(SPAN - 1):
        for k in range(PARTS):
            departed(part(n, k), ("halo", n, k))
    for k in range(NZ - 1):
        departed(piece_q(k), ("zq", k))
        departed(piece_s(k), ("zs", k))
    per_core(drain)

    for k in range(PARTS):
        departed(part(SPAN - 1, k), ("halo", SPAN - 1, k))


def run_whole(lengths, ids, slots, inverse, tokens, qkv_weight, out_weight, down, up):
    anywhere = pl.BlockSpec(memory_space=pl.ANY)
    scalar = pl.BlockSpec(memory_space=pltpu.SMEM)
    return pl.pallas_call(
        whole_kernel,
        out_shape=jax.ShapeDtypeStruct((TOK, 2 * WIDTH), bf16),
        in_specs=[scalar] * 2 + [pl.BlockSpec(memory_space=pltpu.VMEM)] * 2 + [anywhere] * 5,
        out_specs=anywhere,
        scratch_shapes=[
            pltpu.VMEM((2, NX, 3, 2048, 128), bf16),
            pltpu.VMEM((2, NX, 3, 1024, 256), bf16),
            pltpu.VMEM((SPAN + 1, TOK, 2048), bf16),
            pltpu.VMEM((2, HEADS, TOK, HS), bf16),
            pltpu.VMEM((HEADS, TOK, HS), bf16),
            pltpu.VMEM((HEADS, TOK, HS), bf16),
            pltpu.VMEM((256, 1024), bf16),
            pltpu.VMEM((256, 2048), bf16),
            pltpu.VMEM((256, 2048), bf16),
            pltpu.VMEM((TOK, 256), bf16),
            pltpu.VMEM((HEADS, TOK, HS), f32),
            pltpu.VMEM((2, HEADS, TOK, HS), f32),
            pltpu.VMEM((HEADS, TOK, 128), f32),
            pltpu.VMEM((HEADS, TOK, 128), f32),
            pltpu.VMEM((SPAN + 1, TOK, 128), f32),
            pltpu.VMEM((SPAN + 1, TOK, 128), f32),
            pltpu.VMEM((TOK, 128), i32),
            pltpu.VMEM((SPAN + 1, TOK, 128), i32),
            pltpu.VMEM((TOK, TOK), f32),
            pltpu.VMEM((TOK, 2 * WIDTH), bf16),
            pltpu.VMEM((TOK, WIDTH), bf16),
            pltpu.SemaphoreType.DMA((200,)),
            pltpu.SemaphoreType.DMA((200,)),
            pltpu.SemaphoreType.DMA((8,)),
            pltpu.SemaphoreType.DMA((8,)),
        ],
        compiler_params=pltpu.CompilerParams(
            collective_id=0, has_side_effects=True, vmem_limit_bytes=63 * 1024 * 1024
        ),
    )(lengths, ids, slots, inverse, tokens, qkv_weight, out_weight, down, up)


def per_device(
    tokens, qkv_weight, out_weight, adapter_down, adapter_up, lengths, adapter_ids, adapter_slot
):
    rotary = HS // 4
    inverse = 10000.0 ** (-2.0 * (np.arange(128) % (rotary // 2)) / rotary)
    inverse = jnp.asarray(np.tile(inverse[None, :], (8, 1)), f32)
    return run_whole(
        lengths, adapter_ids, adapter_slot.reshape(1, -1), inverse, tokens, qkv_weight, out_weight,
        adapter_down.reshape(-1, 2048), adapter_up.reshape(-1, 2048),
    )


def solution(mesh):
    in_specs = (
        P(("fsdp", "seq"), None),
        P("seq", "fsdp"),
        P("seq", "fsdp"),
        P("seq", None, None),
        P("seq", None, None),
        P(),
        P(),
        P(),
    )
    out_specs = P(("fsdp", "seq"), None)
    return jax.shard_map(
        per_device, mesh=mesh, in_specs=in_specs, out_specs=out_specs, check_vma=False
    )
```
